32 devices in a mesh: seq: 4 (over z), fsdp: 8 (over y, x, core).
Axes of the slice: x: 2, y: 2, z: 4, core: 2. Of those that a mesh axis runs over, the one named last changes fastest.
Arguments:
- tokens: bfloat16 [2, 8, 256, 2048], P(None, 'fsdp', 'seq'), may hold values from -6 to 6
- lengths: int32 [2, 8, 4], P(None, 'fsdp'), may hold values from 1 to 128, 256 in all within a row
- in_weight: bfloat16 [2048, 12288], P(('seq', 'fsdp')), may hold values from -0.125 to 0.125
- decay_weight: bfloat16 [2048, 32], P(('seq', 'fsdp')), may hold values from -0.125 to 0.125
- conv_weight: bfloat16 [8192, 4], P(('seq', 'fsdp')), may hold values from -3 to 3
- a_log: float32 [16], replicated, may hold values from -4 to 0.5
- dt_bias: float32 [16], replicated, may hold values from -1.5 to 1
- norm_gains: bfloat16 [2, 2048], P(None, ('seq', 'fsdp')), may hold values from 0.5 to 1.5
- out_gain: float32 [256], replicated, may hold values from 0.5 to 1.5
- out_weight: bfloat16 [4096, 2048], P(('seq', 'fsdp')), may hold values from -0.1875 to 0.1875
- up_weight: bfloat16 [2048, 11008], P(('seq', 'fsdp')), may hold values from -0.125 to 0.125
- down_weight: bfloat16 [5504, 2048], P(('seq', 'fsdp')), may hold values from -0.15625 to 0.15625
- cotangent: bfloat16 [2, 8, 256, 2048], P(None, 'fsdp', 'seq'), may hold values from -6 to 6
Outputs:
- block_out: bfloat16 [2, 8, 256, 2048], P(None, 'fsdp', 'seq')
- grad_tokens: float32 [2, 8, 256, 2048], P(None, 'fsdp', 'seq')
- grad_in: float32 [2048, 12288], P(('seq', 'fsdp'))
- grad_decay: float32 [2048, 32], P(('seq', 'fsdp'))
- grad_conv: float32 [8192, 4], P(('seq', 'fsdp'))
- grad_a_log: float32 [16], replicated
- grad_dt_bias: float32 [16], replicated
- grad_norm_gains: float32 [2, 2048], P(None, ('seq', 'fsdp'))
- grad_out_gain: float32 [256], replicated
- grad_out: float32 [4096, 2048], P(('seq', 'fsdp'))
- grad_up: float32 [2048, 11008], P(('seq', 'fsdp'))
- grad_down: float32 [5504, 2048], P(('seq', 'fsdp'))
The draws below stay inside these ranges and needn't reach their ends.
Inputs may be any that keep to these rules, and one draw needn't show every extreme that they name: Each pack's 4 lengths sum to 256; in each pack the longest document has exactly 128 tokens.
All inputs are finite; a program needn't handle non-finite values.
Results may differ from the reference program's by a relative error of at most 0.017.
Values may be sent and summed in bfloat16 or wider, within the bound.
No kernel may reach another device: no remote copies, remote signals or barrier semaphores. Data moves between devices by JAX's collectives and lax.ppermute only.
A program may use at most 512 MiB of HBM per device.

```python
import math
import jax
import jax.numpy as jnp
import numpy as np
from jax import lax

D = 2048
H = 16
DK = 128
DV = 256
FF = 5504
CONV = 4
GROUP = 64
MICRO = 2
DOCS = 4
PACK = 256
PACKS = 8


def block_scale(key, shape, pieces, low, top_value):
    level, own = 1.0, jax.random.fold_in(key, 6)
    for position, blocks in pieces:
        draws = jnp.exp(jax.random.uniform(jax.random.fold_in(own, position), (blocks,), jnp.float32, low / len(pieces), top_value / len(pieces)))
        level = level * jnp.repeat(draws, shape[position] // blocks).reshape([-1 if axis == position else 1 for axis in range(len(shape))])
    return level


def profile(count, total, limit, slope):
    portions = [(1 << 20) // math.isqrt(standing ** slope) + 1 for standing in range(2, count + 1)]
    surplus, holding = total - limit - (count - 1), [1] * (count - 1)
    while surplus > 0:
        candidates = [i for i in range(count - 1) if holding[i] < limit]
        whole, budget = sum([portions[i] for i in candidates]), surplus
        for i in candidates:
            more = min(limit - holding[i], max(1, budget * portions[i] // whole), surplus)
            holding[i] = holding[i] + more
            surplus = surplus - more
    return np.array([limit] + holding)


def uneven_parts(key, amount, total, reach, slope):
    if amount == 2:
        one = jax.random.randint(key, (), max(1, total - reach), min(reach, total - 1) + 1)
        return jnp.stack([one, total - one])
    tallies = jnp.asarray(profile(amount, total, reach, slope), jnp.int32)
    couples = (amount - 1) // 2
    source_of, taker = tallies[1:1 + 2 * couples:2], tallies[2:2 + 2 * couples:2]
    margin = jnp.minimum(source_of - 1, reach - taker)
    passed = jax.random.randint(jax.random.fold_in(key, 1), (couples,), 0, 1 << 20) % (margin + 1)
    tallies = tallies.at[1:1 + 2 * couples:2].set(source_of - passed).at[2:2 + 2 * couples:2].set(taker + passed)
    return tallies[jax.random.permutation(jax.random.fold_in(key, 2), amount)]


def normal_values(own_key, shape, deviation, bound, shards=(), kind=jnp.bfloat16):
    values = deviation * jax.random.normal(own_key, shape, jnp.float32)
    if shards:
        values = values * block_scale(own_key, shape, shards, -0.22, 0.18)
    return jnp.clip(values, -bound, bound).astype(kind)


def setup_inputs(seed: int = 0) -> dict:
    key_list = jax.random.split(jax.random.key(seed), 14)
    tokens = normal_values(key_list[0], (MICRO, PACKS, PACK, D), 1.0, 6.0, ((1, 8), (2, 4)))
    lengths = jax.vmap(lambda own: uneven_parts(own, DOCS, PACK, PACK // 2, 2))(jax.random.split(key_list[1], MICRO * PACKS)).reshape((MICRO, PACKS, DOCS)).astype(jnp.int32)
    in_weight = normal_values(key_list[2], (D, 2 * H * DK + 2 * H * DV), D ** -0.5, 0.125, ((0, 32),))
    decay_weight = normal_values(key_list[3], (D, 2 * H), D ** -0.5, 0.125, ((0, 32),))
    conv_weight = normal_values(key_list[4], (2 * H * DK + H * DV, CONV), CONV ** -0.5, 3.0, ((0, 32),))
    a_log = jnp.clip(jax.random.uniform(key_list[5], (H,), jnp.float32, -4.0, 0.5), -4.0, 0.5)
    dt_bias = jnp.clip(jax.random.uniform(key_list[6], (H,), jnp.float32, -1.5, 1.0), -1.5, 1.0)
    norm_gains = jnp.clip(1.0 + 0.1 * jax.random.normal(key_list[7], (2, D), jnp.float32), 0.5, 1.5).astype(jnp.bfloat16)
    out_gain = jnp.clip(1.0 + 0.1 * jax.random.normal(key_list[8], (DV,), jnp.float32), 0.5, 1.5)
    out_weight = normal_values(key_list[9], (H * DV, D), (H * DV // 4) ** -0.5, 0.1875, ((0, 32),))
    up_weight = normal_values(key_list[10], (D, 2 * FF), D ** -0.5, 0.125, ((0, 32),))
    down_weight = normal_values(key_list[11], (FF, D), (FF // 4) ** -0.5, 0.15625, ((0, 32),))
    cotangent = normal_values(key_list[12], (MICRO, PACKS, PACK, D), 1.0, 6.0, ((1, 8), (2, 4)))
    return dict(tokens=tokens, lengths=lengths, in_weight=in_weight, decay_weight=decay_weight, conv_weight=conv_weight, a_log=a_log, dt_bias=dt_bias, norm_gains=norm_gains, out_gain=out_gain, out_weight=out_weight, up_weight=up_weight, down_weight=down_weight, cotangent=cotangent)


@jax.custom_vjp
def low(v):
    return lax.optimization_barrier(v.astype(jnp.bfloat16)).astype(jnp.float32)

@jax.custom_vjp
def low_back(v):
    return v

def low_keep(v):
    return (low(v), None)

def low_pass(kept, grad):
    return (grad,)

def back_keep(v):
    return (v, None)

def back_low(kept, grad):
    return (low(grad),)
low.defvjp(low_keep, low_pass)
low_back.defvjp(back_keep, back_low)
epsilon = 1e-06

def product(left, right):
    return jnp.dot(left, right, precision=lax.Precision.HIGHEST, preferred_element_type=jnp.float32)

def precise_total(form, left, right):
    return jnp.einsum(form, left, right, precision=lax.Precision.HIGHEST, preferred_element_type=jnp.float32)

def rms_apply(values, gain):
    return values * lax.rsqrt(lax.optimization_barrier(jnp.mean(values * values, axis=-1, keepdims=True)) + epsilon) * gain

def unit_rows(values):
    return values * lax.rsqrt(lax.optimization_barrier(jnp.sum(values * values, axis=-1, keepdims=True)) + epsilon)

def segment_ids(lengths_row, count):
    ends = jnp.cumsum(lengths_row, dtype=jnp.int32)[:-1].astype(jnp.int32)
    places = jnp.arange(count, dtype=jnp.int32)
    return lax.optimization_barrier(jnp.sum((places[:, None] >= ends[None, :]).astype(jnp.int32), axis=1, dtype=jnp.int32)).astype(jnp.int32)

def short_conv(values, weight, segs):
    total = values * weight[:, CONV - 1]
    for lag in range(1, CONV):
        moved = jnp.concatenate([jnp.zeros((lag, values.shape[1]), jnp.float32), values[:-lag]], axis=0)
        earlier = jnp.concatenate([jnp.full((lag,), -1, jnp.int32), segs[:-lag]], axis=0)
        same = jnp.where(earlier == segs, 1.0, 0.0).astype(jnp.float32)
        total = total + moved * same[:, None] * weight[:, CONV - 1 - lag]
    return total

def delta_rule(query, keys, values, rate, beta):
    count = query.shape[0]
    blocks = count // GROUP

    def token_step(state_matrix, item):
        current_query, current_key, current_value, rate_now, current_beta_rate = item
        held_state = state_matrix * rate_now[:, None, None]
        estimate_value = precise_total('ni,nij->nj', current_key, held_state)
        state_matrix = held_state + precise_total('bd,by->bdy', current_key, current_beta_rate[:, None] * (current_value - estimate_value))
        return (state_matrix, precise_total('ni,nij->nj', current_query, state_matrix))

    def block_step(state_matrix, item):
        return lax.scan(token_step, state_matrix, item)

    def split(array):
        return array.reshape((blocks, GROUP) + array.shape[1:])
    start = jnp.zeros((H, DK, DV), jnp.float32)
    items = tuple((split(array) for array in (query, keys, values, rate, beta)))
    _, outputs = lax.scan(jax.checkpoint(block_step), start, items)
    return outputs.reshape(count, H, DV)

def head_mix(sent, pairs, conv_weight, a_log, dt_bias, segs):
    count = sent.shape[0]
    conv = jax.nn.silu(short_conv(sent, conv_weight, segs))
    query = unit_rows(conv[:, :H * DK].reshape(count, H, DK)) * DK ** (-0.5)
    keys = unit_rows(conv[:, H * DK:2 * H * DK].reshape(count, H, DK))
    values = conv[:, 2 * H * DK:].reshape(count, H, DV)
    pair_view = pairs.reshape(count, H, 2)
    logdecay = -jnp.exp(a_log) * jax.nn.softplus(pair_view[:, :, 0] + dt_bias)
    beta = jax.nn.sigmoid(pair_view[:, :, 1])
    earlier = jnp.concatenate([jnp.full((1,), -1, jnp.int32), segs[:-1]], axis=0)
    keep = jnp.where(earlier == segs, 1.0, 0.0).astype(jnp.float32)
    rate = keep[:, None] * jnp.exp(logdecay)
    return delta_rule(query, keys, values, rate, beta).reshape(count, H * DV)

def pack_forward(inputs, lengths_row, params):
    in_w, decay_w, conv_w, a_log, dt_bias, gains, out_gain, out_w, up_w, down_w = params
    segs = segment_ids(lengths_row, inputs.shape[0])
    split = 2 * H * DK + H * DV
    first = low(rms_apply(inputs, gains[0]))
    proj = product(first, in_w)
    sent = low_back(low(proj[:, :split]))
    gate_out = low_back(proj[:, split:])
    pairs = low_back(low(product(first, decay_w)))
    mixed = low_back(low(head_mix(sent, pairs, conv_w, a_log, dt_bias, segs)))
    heads = mixed.reshape(inputs.shape[0], H, DV)
    normed = low(rms_apply(heads, out_gain).reshape(inputs.shape[0], H * DV) * jax.nn.silu(gate_out))
    branch = low_back(product(normed, out_w))
    middle = inputs + branch
    second = low(rms_apply(middle, gains[1]))
    both = low_back(product(second, up_w))
    act = low(jax.nn.silu(both[:, :FF]) * both[:, FF:])
    return middle + product(act, down_w)

def reference(tokens, lengths, in_weight, decay_weight, conv_weight, a_log, dt_bias, norm_gains, out_gain, out_weight, up_weight, down_weight, cotangent):
    params = tuple((array.astype(jnp.float32) for array in (in_weight, decay_weight, conv_weight, a_log, dt_bias, norm_gains, out_gain, out_weight, up_weight, down_weight)))
    flat_tokens = tokens.reshape(MICRO * PACKS, PACK, D).astype(jnp.float32)
    flat_lengths = lengths.reshape(MICRO * PACKS, DOCS)

    def forward(inputs, weights):

        def step(carry, item):
            return (carry, jax.checkpoint(pack_forward)(item[0], item[1], weights))
        _, outputs = lax.scan(step, jnp.zeros((), jnp.float32), (inputs, flat_lengths))
        return outputs
    outputs, pullback = jax.vjp(forward, flat_tokens, params)
    grad_inputs, grads = pullback(cotangent.reshape(MICRO * PACKS, PACK, D).astype(jnp.float32))
    shape = (MICRO, PACKS, PACK, D)
    return (outputs.reshape(shape).astype(jnp.bfloat16), grad_inputs.reshape(shape), grads[0], grads[1], grads[2], grads[3], grads[4], grads[5], grads[6], grads[7], grads[8], grads[9])
```

```python
from functools import partial

import jax
import jax.numpy as jnp
from jax import lax
from jax.experimental import pallas as pl
from jax.experimental.layout import Layout, with_layout_constraint
from jax.experimental.pallas import tpu as pltpu
from jax.sharding import PartitionSpec as P

D = 2048
H = 16
DK = 128
DV = 256
FF = 5504
CONV = 4
EPS = 1e-06
BLOCK = 128
LANES = 128
F32 = jnp.float32
BF16 = jnp.bfloat16


def round_up(value, step):
    return -(-value // step) * step


NN = (((1,), (0,)), ((), ()))
NT = (((1,), (1,)), ((), ()))
TN = (((0,), (0,)), ((), ()))


def dot1(left, right, form=NN):
    return lax.dot_general(
        left.astype(BF16), right.astype(BF16), form, preferred_element_type=F32
    )


def halves(value):
    high = value.astype(BF16)
    return high, (value - high.astype(F32)).astype(BF16)


def dot3(left, right, form=NN):
    left_high, left_low = halves(left)
    right_high, right_low = halves(right)
    dot = partial(lax.dot_general, dimension_numbers=form, preferred_element_type=F32)
    return dot(left_high, right_high) + (dot(left_high, right_low) + dot(left_low, right_high))


def sigmoid(value):
    return 1.0 / (1.0 + jnp.exp(-value))


def pack_masks(ends, count):
    place = lax.broadcasted_iota(jnp.int32, (count, 1), 0)
    start = jnp.zeros((count, 1), jnp.int32)
    for end in ends:
        start = jnp.where(place >= end, jnp.maximum(start, end), start)
    rows = lax.broadcasted_iota(jnp.int32, (count, count), 0)
    cols = lax.broadcasted_iota(jnp.int32, (count, count), 1)
    return place, start, rows, cols


def conv_silu(raw, taps, place, start):
    total = raw * taps[CONV - 1 : CONV]
    for lag in range(1, CONV):
        moved = pltpu.roll(raw, lag, 0)
        same = place - lag >= start
        total = total + jnp.where(same, moved, 0.0) * taps[CONV - 1 - lag : CONV - lag]
    gate = sigmoid(total)
    return total, gate, total * gate


def conv_silu_back(grad, total, gate, raw, taps, place, start):
    grad_total = grad * gate * (1.0 + total * (1.0 - gate))
    grad_raw = grad_total * taps[CONV - 1 : CONV]
    grad_taps = [None] * CONV
    grad_taps[CONV - 1] = jnp.sum(grad_total * raw, axis=0, keepdims=True)
    count = raw.shape[0]
    for lag in range(1, CONV):
        same = place - lag >= start
        kept = jnp.where(same, grad_total, 0.0)
        moved = pltpu.roll(raw, lag, 0)
        grad_taps[CONV - 1 - lag] = jnp.sum(kept * moved, axis=0, keepdims=True)
        grad_raw = grad_raw + pltpu.roll(kept, count - lag, 0) * taps[CONV - 1 - lag : CONV - lag]
    return grad_raw, grad_taps


def unit_rows(values):
    scale = lax.rsqrt(jnp.sum(values * values, axis=1, keepdims=True) + EPS)
    return values * scale, scale


def unit_rows_back(grad, values, scale):
    inner = jnp.sum(values * grad, axis=1, keepdims=True)
    return scale * grad - values * (scale * scale * scale * inner)


def column(values, lanes, index):
    return jnp.sum(jnp.where(lanes == index, values, 0.0), axis=1, keepdims=True)


def decay_grid(log_rate, start, rows, cols):
    count = log_rate.shape[0]
    lower = jnp.where(cols <= rows, 1.0, 0.0).astype(BF16)
    spread = jnp.where(cols < rows, jnp.broadcast_to(log_rate, (count, count)), 0.0)
    first = spread.astype(BF16)
    rest = spread - first.astype(F32)
    second = rest.astype(BF16)
    third = (rest - second.astype(F32)).astype(BF16)
    dot = partial(lax.dot_general, dimension_numbers=NN, preferred_element_type=F32)
    summed = dot(lower, first) + (dot(lower, second) + dot(lower, third))
    inside = (cols <= rows) & (cols >= start)
    return jnp.where(inside, jnp.exp(jnp.where(inside, summed, 0.0)), 0.0)


def unit_lower_inverse(strict):
    size = strict.shape[0]
    rows = lax.broadcasted_iota(jnp.int32, (size, size), 0)
    cols = lax.broadcasted_iota(jnp.int32, (size, size), 1)
    result = jnp.where(rows == cols, 1.0, 0.0).astype(F32)
    level = 0
    while (1 << level) < size:
        width = 1 << level
        joint = (
            ((rows >> (level + 1)) == (cols >> (level + 1)))
            & ((rows & width) != 0)
            & ((cols & width) == 0)
        )
        part = jnp.where(joint, strict, 0.0)
        if level == 0:
            result = result - part
        else:
            result = result - dot3(result, dot3(part, result))
        level += 1
    return result


def read_rows(ref, offset, width):
    shape = ref.shape
    return ref[:, 0, :, pl.ds(offset, width)].reshape(shape[0] * shape[2], width)


def write_rows(ref, offset, value):
    shape = ref.shape
    ref[:, 0, :, pl.ds(offset, value.shape[1])] = value.reshape(
        shape[0], shape[2], value.shape[1]
    ).astype(ref.dtype)


def pack_ends(lengths_ref, micro, docs):
    ends, total = [], 0
    for index in range(docs - 1):
        total = total + lengths_ref[micro, index]
        ends.append(total)
    return ends


def head_inputs(sent_ref, taps_ref, rate_ref, head, heads, place, start):
    qw = heads * DK
    out = {}
    for name, offset, width in (
        ("q", head * DK, DK),
        ("k", qw + head * DK, DK),
        ("v", 2 * qw + head * DV, DV),
    ):
        offset = pl.multiple_of(offset, LANES)
        raw = read_rows(sent_ref, offset, width).astype(F32)
        taps = taps_ref[:, pl.ds(offset, width)]
        out[name] = (offset, raw, taps) + conv_silu(raw, taps, place, start)
    offset = 2 * qw + heads * DV
    pairs = read_rows(sent_ref, offset, LANES).astype(F32)
    lanes = lax.broadcasted_iota(jnp.int32, pairs.shape, 1)
    decay_in = column(pairs, lanes, 2 * head) + rate_ref[1, head]
    soft = jnp.maximum(decay_in, 0.0) + jnp.log1p(jnp.exp(-jnp.abs(decay_in)))
    out["log"] = rate_ref[0, head] * soft
    out["decay_in"] = decay_in
    out["beta"] = sigmoid(column(pairs, lanes, 2 * head + 1))
    out["lanes"] = lanes
    return out


def mixer_forward_kernel(
    micro, per_step, heads, docs, lengths_ref, rate_ref, sent_ref, taps_ref,
    mixed_ref, update_ref, inverse_ref,
):
    count = sent_ref.shape[0] * sent_ref.shape[2]
    place, start, rows, cols = pack_masks(pack_ends(lengths_ref, micro, docs), count)
    blocks = count // BLOCK
    for local in range(per_step):
        head = pl.program_id(0) * per_step + local
        made = head_inputs(sent_ref, taps_ref, rate_ref, head, heads, place, start)
        query = unit_rows(made["q"][5])[0] * DK ** (-0.5)
        keys = unit_rows(made["k"][5])[0]
        values = made["v"][5]
        beta = made["beta"]
        decay = decay_grid(made["log"], start, rows, cols)
        system = jnp.where(cols < rows, decay, 0.0) * beta * dot3(keys, keys, NT)
        target = beta * values
        updates = []
        for block in range(blocks):
            at = slice(block * BLOCK, (block + 1) * BLOCK)
            inverse = unit_lower_inverse(system[at, at])
            inverse_ref[local, block] = inverse
            right = target[at]
            for earlier in range(block):
                right = right - dot3(
                    system[at, earlier * BLOCK : (earlier + 1) * BLOCK], updates[earlier]
                )
            updates.append(dot3(inverse, right))
        update = jnp.concatenate(updates, axis=0)
        update_ref[local] = update
        scores = decay * dot1(query, keys, NT)
        write_rows(mixed_ref, pl.multiple_of(head * DV, LANES), dot1(scores, update))


def mixer_backward_kernel(
    micro, per_step, heads, docs, lengths_ref, rate_ref, sent_ref, taps_ref,
    update_ref, inverse_ref, grad_ref,
    grad_sent_ref, grad_taps_ref, small_ref,
):
    count = sent_ref.shape[0] * sent_ref.shape[2]
    place, start, rows, cols = pack_masks(pack_ends(lengths_ref, micro, docs), count)
    blocks = count // BLOCK
    pair_offset = 2 * heads * DK + heads * DV

    @pl.when(pl.program_id(0) == 0)
    def _():
        small_ref[...] = jnp.zeros_like(small_ref)
        grad_taps_ref[...] = jnp.zeros_like(grad_taps_ref)
        write_rows(grad_sent_ref, pair_offset, jnp.zeros((count, LANES), BF16))

    grad_pairs = read_rows(grad_sent_ref, pair_offset, LANES).astype(F32)
    small_lanes = lax.broadcasted_iota(jnp.int32, (1, LANES), 1)
    for local in range(per_step):
        head = pl.program_id(0) * per_step + local
        made = head_inputs(sent_ref, taps_ref, rate_ref, head, heads, place, start)
        unit_q, scale_q = unit_rows(made["q"][5])
        query = unit_q * DK ** (-0.5)
        keys, scale_k = unit_rows(made["k"][5])
        values = made["v"][5]
        beta = made["beta"]
        grad_mixed = read_rows(grad_ref, pl.multiple_of(head * DV, LANES), DV)
        decay = decay_grid(made["log"], start, rows, cols)
        strict = jnp.where(cols < rows, decay, 0.0)
        keys_keys = dot3(keys, keys, NT)
        weighted = strict * beta
        system = weighted * keys_keys
        scores = decay * dot1(query, keys, NT)
        update = update_ref[local]
        grad_scores = dot1(grad_mixed, update, NT)
        grad_update = dot1(scores, grad_mixed, TN)
        grad_targets = [None] * blocks
        for block in reversed(range(blocks)):
            at = slice(block * BLOCK, (block + 1) * BLOCK)
            right = grad_update[at]
            for later in range(block + 1, blocks):
                right = right - dot3(
                    system[later * BLOCK : (later + 1) * BLOCK, at], grad_targets[later], TN
                )
            grad_targets[block] = dot3(inverse_ref[local, block], right, TN)
        grad_target = jnp.concatenate(grad_targets, axis=0)
        grad_system = -dot1(grad_target, update, NT)
        grad_values = beta * grad_target
        grad_beta = jnp.sum(grad_target * values, axis=1, keepdims=True) + jnp.sum(
            grad_system * strict * keys_keys, axis=1, keepdims=True
        )
        grad_kk = grad_system * weighted
        grad_qk = grad_scores * decay
        grad_query = dot1(grad_qk, keys) * DK ** (-0.5)
        grad_keys = dot1(grad_kk, keys) + dot1(grad_kk, keys, TN) + dot1(grad_qk, query, TN)
        grad_spread = grad_scores * scores + grad_system * system
        lower = jnp.where(cols <= rows, 1.0, 0.0).astype(BF16)
        high, low = halves(grad_spread)
        dot = partial(lax.dot_general, dimension_numbers=TN, preferred_element_type=F32)
        after = dot(lower, high) + dot(lower, low)
        grad_log = jnp.sum(jnp.where(cols < rows, after, 0.0), axis=1, keepdims=True)
        grad_decay = grad_log * rate_ref[0, head] * sigmoid(made["decay_in"])
        grad_beta_in = grad_beta * beta * (1.0 - beta)
        lanes = made["lanes"]
        grad_pairs = jnp.where(lanes == 2 * head, grad_decay, grad_pairs)
        grad_pairs = jnp.where(lanes == 2 * head + 1, grad_beta_in, grad_pairs)
        grad_alog = jnp.sum(grad_log * made["log"], axis=0, keepdims=True)
        grad_dt = jnp.sum(grad_decay, axis=0, keepdims=True)
        small_ref[0:1] += jnp.where(small_lanes == head, grad_alog, 0.0)
        small_ref[1:2] += jnp.where(small_lanes == head, grad_dt, 0.0)
        for name, grad in (
            ("q", unit_rows_back(grad_query, made["q"][5], scale_q)),
            ("k", unit_rows_back(grad_keys, made["k"][5], scale_k)),
            ("v", grad_values),
        ):
            where, raw, taps, total, opened, _ = made[name]
            grad_raw, grad_taps = conv_silu_back(grad, total, opened, raw, taps, place, start)
            write_rows(grad_sent_ref, where, grad_raw)
            for tap in range(CONV):
                grad_taps_ref[tap : tap + 1, pl.ds(where, raw.shape[1])] += grad_taps[tap]
    write_rows(grad_sent_ref, pair_offset, grad_pairs)


def gate_forward_kernel(heads, mixed_ref, gate_ref, gain_ref, normed_ref):
    for head in range(heads):
        offset = head * DV
        mixed = read_rows(mixed_ref, offset, DV).astype(F32)
        gate = read_rows(gate_ref, offset, DV)
        scale = lax.rsqrt(jnp.mean(mixed * mixed, axis=1, keepdims=True) + EPS)
        write_rows(normed_ref, offset, mixed * scale * gain_ref[...] * (gate * sigmoid(gate)))


def gate_backward_kernel(
    heads, mixed_ref, gate_ref, gain_ref, grad_ref, grad_mixed_ref, grad_gate_ref, grad_gain_ref
):
    @pl.when(pl.program_id(0) == 0)
    def _():
        grad_gain_ref[...] = jnp.zeros_like(grad_gain_ref)

    gain = gain_ref[...]
    for head in range(heads):
        offset = head * DV
        mixed = read_rows(mixed_ref, offset, DV).astype(F32)
        gate = read_rows(gate_ref, offset, DV)
        grad = read_rows(grad_ref, offset, DV)
        scale = lax.rsqrt(jnp.mean(mixed * mixed, axis=1, keepdims=True) + EPS)
        soft = sigmoid(gate)
        plain_rows = mixed * scale
        write_rows(
            grad_gate_ref, offset, grad * plain_rows * gain * soft * (1.0 + gate * (1.0 - soft))
        )
        grad = grad * (gate * soft)
        grad_gain_ref[...] += jnp.sum(grad * plain_rows, axis=0, keepdims=True)
        grad = grad * gain
        inner = jnp.mean(mixed * grad, axis=1, keepdims=True)
        write_rows(
            grad_mixed_ref, offset, scale * grad - mixed * (scale * scale * scale * inner)
        )


def row_spec(array, micro):
    spans, micros, length, width = array.shape
    pick = micro if micros > 1 else 0
    return pl.BlockSpec((spans, 1, length, width), lambda h: (0, pick, 0, 0))


def span_spec(array, micro):
    _, micros, length, width = array.shape
    pick = micro if micros > 1 else 0
    return pl.BlockSpec((1, 1, length, width), lambda s: (s, pick, 0, 0))


def whole_spec(*dims):
    return pl.BlockSpec(dims, lambda h: (0,) * len(dims))


def mixer_cost(sent, heads, passes):
    count = sent.shape[0] * sent.shape[2]
    return pl.CostEstimate(
        flops=passes * heads * 2 * count * count * DV,
        bytes_accessed=passes * heads * count * count * 4,
        transcendentals=heads * count * count,
    )


def mixer_forward(micro, lengths, rates, sent, taps, heads):
    spans, _, length, width = sent.shape
    count, per_step = spans * length, 2 if heads % 2 == 0 else 1
    blocks = count // BLOCK
    smem = pl.BlockSpec(memory_space=pltpu.SMEM)
    mixed = jax.ShapeDtypeStruct((spans, 1, length, heads * DV), BF16)
    return pl.pallas_call(
        partial(mixer_forward_kernel, micro, per_step, heads, lengths.shape[1]),
        grid=(heads // per_step,),
        in_specs=[smem, smem, row_spec(sent, micro), whole_spec(CONV, width)],
        out_specs=[
            row_spec(mixed, 0),
            pl.BlockSpec((per_step, count, DV), lambda h: (h, 0, 0)),
            pl.BlockSpec((per_step, blocks, BLOCK, BLOCK), lambda h: (h, 0, 0, 0)),
        ],
        out_shape=[
            mixed,
            jax.ShapeDtypeStruct((heads, count, DV), F32),
            jax.ShapeDtypeStruct((heads, blocks, BLOCK, BLOCK), F32),
        ],
        compiler_params=pltpu.CompilerParams(vmem_limit_bytes=40 * 1024 * 1024),
        cost_estimate=mixer_cost(sent, heads, 60),
        name="mixer_forward",
    )(lengths, rates, sent, taps)


def mixer_backward(micro, lengths, rates, sent, taps, update, inverse, grad, heads):
    spans, _, length, width = sent.shape
    count, per_step = spans * length, 2 if heads % 2 == 0 else 1
    blocks = count // BLOCK
    smem = pl.BlockSpec(memory_space=pltpu.SMEM)
    grad_sent = jax.ShapeDtypeStruct((spans, 1, length, width), BF16)
    return pl.pallas_call(
        partial(mixer_backward_kernel, micro, per_step, heads, lengths.shape[1]),
        grid=(heads // per_step,),
        in_specs=[
            smem, smem, row_spec(sent, micro), whole_spec(CONV, width),
            pl.BlockSpec((per_step, count, DV), lambda h: (h, 0, 0)),
            pl.BlockSpec((per_step, blocks, BLOCK, BLOCK), lambda h: (h, 0, 0, 0)),
            row_spec(grad, 0),
        ],
        out_specs=[row_spec(grad_sent, 0), whole_spec(CONV, width), whole_spec(8, LANES)],
        out_shape=[
            grad_sent,
            jax.ShapeDtypeStruct((CONV, width), F32),
            jax.ShapeDtypeStruct((8, LANES), F32),
        ],
        compiler_params=pltpu.CompilerParams(vmem_limit_bytes=40 * 1024 * 1024),
        cost_estimate=mixer_cost(sent, heads, 40),
        name="mixer_backward",
    )(lengths, rates, sent, taps, update, inverse, grad)


def gate_forward(micro, mixed, gate, gain, heads):
    return pl.pallas_call(
        partial(gate_forward_kernel, heads),
        grid=(mixed.shape[0],),
        in_specs=[span_spec(mixed, 0), span_spec(gate, micro), whole_spec(1, DV)],
        out_specs=span_spec(mixed, 0),
        out_shape=jax.ShapeDtypeStruct(mixed.shape, BF16),
        cost_estimate=pl.CostEstimate(
            flops=20 * mixed.size, bytes_accessed=8 * mixed.size, transcendentals=mixed.size
        ),
        name="gate_forward",
    )(mixed, gate, gain)


def gate_backward(micro, mixed, gate, gain, grad, heads):
    out = jax.ShapeDtypeStruct(mixed.shape, BF16)
    return pl.pallas_call(
        partial(gate_backward_kernel, heads),
        grid=(mixed.shape[0],),
        in_specs=[
            span_spec(mixed, 0), span_spec(gate, micro), whole_spec(1, DV), span_spec(grad, 0),
        ],
        out_specs=[span_spec(out, 0), span_spec(out, 0), whole_spec(1, DV)],
        out_shape=[out, out, jax.ShapeDtypeStruct((1, DV), F32)],
        cost_estimate=pl.CostEstimate(
            flops=40 * mixed.size, bytes_accessed=14 * mixed.size, transcendentals=mixed.size
        ),
        name="gate_backward",
    )(mixed, gate, gain, grad)


def dot(left, right):
    return jnp.dot(left, right, preferred_element_type=F32)


def outer(left, right):
    return lax.dot_general(left, right, TN, preferred_element_type=F32)


def dot_back(left, right):
    return lax.dot_general(left, right, NT, preferred_element_type=F32)


def after(value, *earlier):
    return lax.optimization_barrier((value,) + earlier)[0]


def plain(array):
    return with_layout_constraint(array, Layout(major_to_minor=tuple(range(array.ndim))))


def exchange(blocks):
    return lax.all_to_all(blocks, "seq", split_axis=0, concat_axis=0, tiled=True)


def gather_rows(rows):
    spans = lax.axis_size("seq")
    return exchange(jnp.broadcast_to(rows[None], (spans,) + rows.shape))


def scatter_rows(partial_rows, spans):
    return exchange(
        partial_rows.astype(BF16).reshape((spans, -1) + partial_rows.shape[1:])
    )


def norm_scale(values):
    return lax.rsqrt(jnp.mean(values * values, axis=-1, keepdims=True) + EPS)


def norm_back(values, gain, grad):
    scale = norm_scale(values)
    inner = gain * grad
    back = scale * inner - values * (
        scale * scale * scale * jnp.mean(values * inner, axis=-1, keepdims=True)
    )
    return back, jnp.sum(values * scale * grad, axis=0)


def shards(
    tokens, lengths, in_weight, decay_weight, conv_weight, a_log, dt_bias, norm_gains, out_gain,
    out_weight, up_weight, down_weight, cotangent,
):
    spans, packs = lax.axis_size("seq"), lax.axis_size("fsdp")
    place = lax.axis_index("seq")
    micros, _, length, _ = tokens.shape
    heads = H // spans
    qw, vw, fw = heads * DK, heads * DV, FF // spans
    fp = round_up(fw, LANES)
    share = in_weight.shape[0]
    local_rows = micros * length

    def columns(array, start, count):
        return array[:, start : start + count * spans].reshape(share, spans, count)

    def widen(array, count):
        return jnp.pad(array, ((0, 0), (0, 0), (0, count - array.shape[2])))

    def by_span(pieces):
        return jnp.concatenate(pieces, axis=2).swapaxes(0, 1)

    def gather_weight(blocks):
        full = plain(lax.all_gather(plain(blocks), "fsdp", axis=1, tiled=True))
        return full.reshape(D, blocks.shape[2])

    conv_share = conv_weight.shape[0]
    conv_cols = CONV * conv_share // share
    small = jnp.concatenate([conv_weight.reshape(share, conv_cols), norm_gains.T], axis=1)
    small = jnp.broadcast_to(small[:, None], (share, spans, conv_cols + 2))
    pairs = jnp.concatenate([decay_weight.reshape(share, spans, 2 * heads), small], axis=2)
    pair_at = 2 * qw + vw
    mix_width = pair_at + LANES
    mix_blocks = by_span([
        columns(in_weight, 0, qw),
        columns(in_weight, H * DK, qw),
        columns(in_weight, 2 * H * DK, vw),
        widen(pairs, LANES),
    ])
    gate_blocks = by_span([columns(in_weight, 2 * H * DK + H * DV, vw)])
    up_blocks = by_span([
        widen(columns(up_weight, 0, fw), fp),
        widen(columns(up_weight, FF, fw), fp),
    ])
    local_tokens = tokens.reshape(local_rows, D)
    local_cot = cotangent.reshape(local_rows, D)
    grouped = (spans, micros, length)
    all_rows = spans * local_rows

    mix_blocks, up_blocks = lax.optimization_barrier((exchange(mix_blocks), up_blocks))
    w_mix = gather_weight(mix_blocks)
    all_tokens = gather_rows(after(local_tokens, mix_blocks))
    gate_blocks = exchange(after(gate_blocks, all_tokens))
    w_gate = gather_weight(after(gate_blocks, w_mix))
    w_out = lax.all_gather(after(out_weight, w_mix), "fsdp", axis=0, tiled=True)

    small = w_mix[:, pair_at + 2 * heads : pair_at + 2 * heads + conv_cols + 2]
    gains = small[:, conv_cols:].T.astype(F32)

    def own(base, width):
        step = conv_share // share
        rows = lax.dynamic_slice_in_dim(
            small[:, :conv_cols], (base + place * width) // step, width // step, axis=0
        )
        return rows.reshape(width, CONV).T

    taps = jnp.concatenate(
        [own(0, qw), own(H * DK, qw), own(2 * H * DK, vw), jnp.zeros((CONV, LANES), BF16)],
        axis=1,
    ).astype(F32)
    rates = jnp.stack([
        -jnp.exp(lax.dynamic_slice_in_dim(a_log, place * heads, heads)),
        lax.dynamic_slice_in_dim(dt_bias, place * heads, heads),
    ])
    gain_row = out_gain.reshape(1, DV)
    pack_lengths = lengths[:, 0]

    inputs = all_tokens.reshape(all_rows, D).astype(F32)
    input_scale = norm_scale(inputs)
    first = (inputs * input_scale * gains[0]).astype(BF16)
    sent = dot(first, w_mix).astype(BF16).reshape(grouped + (mix_width,))
    w_down = lax.all_gather(after(down_weight, sent), "fsdp", axis=0)
    cot = gather_rows(after(local_cot, sent)).reshape(all_rows, D)
    mixers = []
    for micro in range(micros):
        mixers.append(
            mixer_forward(micro, pack_lengths, rates, sent, taps, heads)
        )
        if micro == 0:
            up_blocks = exchange(after(up_blocks, cot, mixers[0][0]))
        sent = after(sent, mixers[-1][0])
    w_down = lax.optimization_barrier(w_down.reshape(fw, D))
    w_up = gather_weight(after(up_blocks, mixers[-1][0]))
    gate = dot(first, w_gate).reshape(grouped + (vw,))
    grad_act = dot_back(cot, w_down).reshape(grouped + (fw,))

    def part(array, micro):
        return array.reshape((micros, length) + array.shape[1:])[micro]

    normeds, branches = [], []
    for micro in range(micros):
        normeds.append(gate_forward(micro, mixers[micro][0], gate, gain_row, heads))
        rows = dot(normeds[-1].reshape(-1, vw), w_out).astype(BF16)
        branches.append(scatter_rows(after(rows, up_blocks), spans))
    middles, seconds = [], []
    for micro in range(micros):
        middle = part(local_tokens, micro).astype(F32) + jnp.sum(
            branches[micro].astype(F32), axis=0
        )
        middles.append(middle)
        seconds.append(gather_rows((middle * norm_scale(middle) * gains[1]).astype(BF16)))

    acts, grad_boths, grad_seconds, sums = [], [], [], [None] * micros
    for micro in range(micros):
        both = dot(seconds[micro].reshape(-1, D), w_up)
        gated, upper = both[:, :fp], both[:, fp:]
        soft = jax.nn.sigmoid(gated)
        acts.append((gated * soft * upper).astype(BF16).reshape(spans, length, fp))
        grad = jnp.pad(grad_act[:, micro].reshape(-1, fw), ((0, 0), (0, fp - fw)))
        grad_both = jnp.concatenate(
            [
                (grad * upper * soft * (1.0 + gated * (1.0 - soft))).astype(BF16),
                (grad * gated * soft).astype(BF16),
            ],
            axis=1,
        )
        grad_boths.append(grad_both.reshape(spans, length, 2 * fp))
        rows = dot_back(grad_both, w_up).astype(BF16)
        grad_seconds.append(scatter_rows(rows, spans))
    act = jnp.stack(acts, axis=1).reshape(all_rows, fp)[:, :fw]
    final_rows = [dot(a.reshape(-1, fp)[:, :fw], w_down).astype(BF16) for a in acts]
    down_grads = outer(act, cot).astype(BF16).reshape(packs, -1, D)
    spare = [final_rows[:1], final_rows[1:] + [down_grads]]
    grad_middles, grad_branches, grad_gain2 = [], [], 0.0
    for micro in range(micros):
        grad_second = jnp.sum(
            after(grad_seconds[micro], *spare[min(micro, 1)]).astype(F32), axis=0
        )
        grad_norm, grad_gain = norm_back(middles[micro], gains[1], grad_second)
        grad_gain2 = grad_gain2 + grad_gain
        grad_middles.append(part(local_cot, micro).astype(F32) + grad_norm)
        grad_branches.append(gather_rows(grad_middles[-1].astype(BF16)))

    def reduce_rows(grad, blocks):
        blocks = plain(grad.astype(BF16).reshape(blocks, -1, grad.shape[1]))
        return plain(lax.psum_scatter(blocks, "fsdp", scatter_dimension=1, tiled=True))

    def joined(blocks, start, width):
        return blocks[:, :, start : start + width].swapaxes(0, 1).astype(F32).reshape(share, -1)

    def all_micros(parts):
        return jnp.stack(parts, axis=1).reshape(all_rows, parts[0].shape[-1])

    up_grads = reduce_rows(
        outer(after(all_micros(seconds), grad_seconds[0]), all_micros(grad_boths)), spans
    )
    finals, waits = [], grad_branches[-1]
    for micro in range(micros):
        waits = scatter_rows(after(final_rows[micro], waits), spans)
        finals.append(middles[micro] + jnp.sum(waits.astype(F32), axis=0))
        sums[micro] = waits
    block_out = jnp.stack(finals).reshape(local_rows, D)

    grad_mixeds, grad_gates, grad_gain = [], [], 0.0
    for micro in range(micros):
        grad = dot_back(grad_branches[micro].reshape(-1, D), w_out)
        grad_mixed, grad_gate, term = gate_backward(
            micro, mixers[micro][0], gate, gain_row,
            grad.reshape(spans, 1, length, vw), heads,
        )
        grad_mixeds.append(grad_mixed)
        grad_gates.append(grad_gate.reshape(spans, length, vw))
        grad_gain = grad_gain + term
    grad_mixeds[0] = after(grad_mixeds[0], up_grads)
    grad_sents, grad_taps, grad_small = [], 0.0, 0.0
    for micro in range(micros):
        _, update, inverse = mixers[micro]
        grad_sent, term_taps, term_small = mixer_backward(
            micro, pack_lengths, rates, sent, taps, update, inverse, grad_mixeds[micro], heads
        )
        if micro + 1 < micros:
            grad_mixeds[micro + 1] = after(grad_mixeds[micro + 1], grad_sent)
        grad_sents.append(grad_sent.reshape(spans, length, mix_width))
        grad_taps, grad_small = grad_taps + term_taps, grad_small + term_small
    grad_proj = all_micros([
        jnp.concatenate(pair, axis=-1) for pair in zip(grad_sents, grad_gates)
    ])
    in_product = outer(after(first, sums[-1]), grad_proj)
    in_grads = reduce_rows(in_product, spans)
    grad_first = dot_back(grad_proj[:, :mix_width], w_mix) + dot_back(
        grad_proj[:, mix_width:], w_gate
    )
    grad_gain1 = jnp.sum(inputs * input_scale * grad_first, axis=0)
    first_rows = grad_first.astype(BF16)
    grad_first = scatter_rows(first_rows, spans)
    out_grads = outer(
        after(all_micros([n[:, 0] for n in normeds]), first_rows), all_micros(grad_branches)
    )
    out_grads = out_grads.astype(BF16).reshape(packs, -1, D)
    down_rows = down_grads.shape[1]
    row_grads = lax.psum_scatter(
        after(jnp.concatenate([out_grads, down_grads], axis=1), in_product),
        "fsdp", scatter_dimension=0,
    ).astype(F32)
    grad_out, grad_down = row_grads[:-down_rows], row_grads[-down_rows:]
    grad_norm1, _ = norm_back(
        local_tokens.astype(F32), gains[0], jnp.sum(grad_first.astype(F32), axis=0)
    )
    grad_tokens = jnp.stack(grad_middles).reshape(local_rows, D) + grad_norm1
    up_grads = exchange(after(up_grads, grad_first))
    in_grads = exchange(after(in_grads, up_grads))
    grad_up = jnp.concatenate([joined(up_grads, 0, fw), joined(up_grads, fp, fw)], axis=1)
    grad_in = jnp.concatenate(
        [
            joined(in_grads, 0, qw),
            joined(in_grads, qw, qw),
            joined(in_grads, 2 * qw, vw),
            joined(in_grads, mix_width, vw),
        ],
        axis=1,
    )
    grad_decay = joined(in_grads, pair_at, 2 * heads)

    gain_rows = jnp.stack([grad_gain1, grad_gain2])
    flat = jnp.concatenate([
        grad_taps[:, :pair_at].reshape(-1), gain_rows.reshape(-1), grad_gain.reshape(-1),
        grad_small[:2].reshape(-1),
    ])
    flat = jnp.pad(flat, (0, round_up(flat.size, 8 * LANES) - flat.size)).reshape(-1, LANES)
    flat = lax.psum(flat, "fsdp")
    flat = lax.all_gather(flat, "seq", axis=0).reshape(spans, -1)
    taps_flat = flat[:, : CONV * pair_at].reshape(spans, CONV, pair_at)

    def all_taps(start, width):
        return taps_flat[:, :, start : start + width].swapaxes(0, 1).reshape(CONV, -1)

    grad_conv = jnp.concatenate(
        [all_taps(0, qw), all_taps(qw, qw), all_taps(2 * qw, vw)], axis=1
    )
    index = place * packs + lax.axis_index("fsdp")
    grad_conv = lax.dynamic_slice_in_dim(grad_conv, index * conv_share, conv_share, axis=1).T
    at = CONV * pair_at
    gains_flat = jnp.sum(flat[:, at : at + 2 * D], axis=0).reshape(2, D)
    gain_share = norm_gains.shape[1]
    grad_gains = lax.dynamic_slice_in_dim(gains_flat, index * gain_share, gain_share, axis=1)
    at = at + 2 * D
    grad_gain = jnp.sum(flat[:, at : at + DV], axis=0)
    at = at + DV
    return (
        block_out.astype(BF16).reshape(micros, 1, length, D),
        grad_tokens.reshape(micros, 1, length, D),
        grad_in,
        grad_decay,
        grad_conv,
        flat[:, at : at + heads].reshape(H),
        flat[:, at + LANES : at + LANES + heads].reshape(H),
        grad_gains,
        grad_gain,
        grad_out,
        grad_up,
        grad_down,
    )


def solution(mesh):
    rows = P(("seq", "fsdp"), None)
    packs = P(None, "fsdp", "seq", None)
    gains = P(None, ("seq", "fsdp"))
    return jax.shard_map(
        shards,
        mesh=mesh,
        in_specs=(
            packs, P(None, "fsdp", None), rows, rows, rows, P(), P(), gains, P(), rows, rows, rows,
            packs,
        ),
        out_specs=(packs, packs, rows, rows, rows, P(), P(), gains, P(), rows, rows, rows),
        check_vma=False,
    )
```

```python
from functools import partial

import jax
import jax.numpy as jnp
from jax import lax
from jax.experimental import pallas as pl
from jax.experimental.layout import Layout, with_layout_constraint
from jax.experimental.pallas import tpu as pltpu
from jax.sharding import PartitionSpec as P

D = 2048
H = 16
DK = 128
DV = 256
FF = 5504
CONV = 4
EPS = 1e-06
BLOCK = 128
LANES = 128
F32 = jnp.float32
BF16 = jnp.bfloat16


def round_up(value, step):
    return -(-value // step) * step


NN = (((1,), (0,)), ((), ()))
NT = (((1,), (1,)), ((), ()))
TN = (((0,), (0,)), ((), ()))


def dot1(left, right, form=NN):
    return lax.dot_general(
        left.astype(BF16), right.astype(BF16), form, preferred_element_type=F32
    )


def halves(value):
    high = value.astype(BF16)
    return high, (value - high.astype(F32)).astype(BF16)


def dot3(left, right, form=NN):
    left_high, left_low = halves(left)
    right_high, right_low = halves(right)
    dot = partial(lax.dot_general, dimension_numbers=form, preferred_element_type=F32)
    return dot(left_high, right_high) + (dot(left_high, right_low) + dot(left_low, right_high))


def sigmoid(value):
    return 1.0 / (1.0 + jnp.exp(-value))


def pack_masks(ends, count):
    place = lax.broadcasted_iota(jnp.int32, (count, 1), 0)
    start = jnp.zeros((count, 1), jnp.int32)
    for end in ends:
        start = jnp.where(place >= end, jnp.maximum(start, end), start)
    rows = lax.broadcasted_iota(jnp.int32, (count, count), 0)
    cols = lax.broadcasted_iota(jnp.int32, (count, count), 1)
    return place, start, rows, cols


def conv_silu(raw, taps, place, start):
    total = raw * taps[CONV - 1 : CONV]
    for lag in range(1, CONV):
        moved = pltpu.roll(raw, lag, 0)
        same = place - lag >= start
        total = total + jnp.where(same, moved, 0.0) * taps[CONV - 1 - lag : CONV - lag]
    gate = sigmoid(total)
    return total, gate, total * gate


def conv_silu_back(grad, total, gate, raw, taps, place, start):
    grad_total = grad * gate * (1.0 + total * (1.0 - gate))
    grad_raw = grad_total * taps[CONV - 1 : CONV]
    grad_taps = [None] * CONV
    grad_taps[CONV - 1] = jnp.sum(grad_total * raw, axis=0, keepdims=True)
    count = raw.shape[0]
    for lag in range(1, CONV):
        same = place - lag >= start
        kept = jnp.where(same, grad_total, 0.0)
        moved = pltpu.roll(raw, lag, 0)
        grad_taps[CONV - 1 - lag] = jnp.sum(kept * moved, axis=0, keepdims=True)
        grad_raw = grad_raw + pltpu.roll(kept, count - lag, 0) * taps[CONV - 1 - lag : CONV - lag]
    return grad_raw, grad_taps


def unit_rows(values):
    scale = lax.rsqrt(jnp.sum(values * values, axis=1, keepdims=True) + EPS)
    return values * scale, scale


def unit_rows_back(grad, values, scale):
    inner = jnp.sum(values * grad, axis=1, keepdims=True)
    return scale * grad - values * (scale * scale * scale * inner)


def column(values, lanes, index):
    return jnp.sum(jnp.where(lanes == index, values, 0.0), axis=1, keepdims=True)


def decay_grid(log_rate, start, rows, cols):
    count = log_rate.shape[0]
    lower = jnp.where(cols <= rows, 1.0, 0.0).astype(BF16)
    spread = jnp.where(cols < rows, jnp.broadcast_to(log_rate, (count, count)), 0.0)
    first = spread.astype(BF16)
    rest = spread - first.astype(F32)
    second = rest.astype(BF16)
    third = (rest - second.astype(F32)).astype(BF16)
    dot = partial(lax.dot_general, dimension_numbers=NN, preferred_element_type=F32)
    summed = dot(lower, first) + (dot(lower, second) + dot(lower, third))
    inside = (cols <= rows) & (cols >= start)
    return jnp.where(inside, jnp.exp(jnp.where(inside, summed, 0.0)), 0.0)


def unit_lower_inverse(strict):
    size = strict.shape[0]
    rows = lax.broadcasted_iota(jnp.int32, (size, size), 0)
    cols = lax.broadcasted_iota(jnp.int32, (size, size), 1)
    result = jnp.where(rows == cols, 1.0, 0.0).astype(F32)
    level = 0
    while (1 << level) < size:
        width = 1 << level
        joint = (
            ((rows >> (level + 1)) == (cols >> (level + 1)))
            & ((rows & width) != 0)
            & ((cols & width) == 0)
        )
        part = jnp.where(joint, strict, 0.0)
        if level == 0:
            result = result - part
        else:
            result = result - dot3(result, dot3(part, result))
        level += 1
    return result


def read_rows(ref, offset, width):
    shape = ref.shape
    return ref[:, 0, :, pl.ds(offset, width)].reshape(shape[0] * shape[2], width)


def write_rows(ref, offset, value):
    shape = ref.shape
    ref[:, 0, :, pl.ds(offset, value.shape[1])] = value.reshape(
        shape[0], shape[2], value.shape[1]
    ).astype(ref.dtype)


def pack_ends(lengths_ref, micro, docs):
    ends, total = [], 0
    for index in range(docs - 1):
        total = total + lengths_ref[micro, index]
        ends.append(total)
    return ends


def head_inputs(sent_ref, taps_ref, rate_ref, head, heads, place, start):
    qw = heads * DK
    out = {}
    for name, offset, width in (
        ("q", head * DK, DK),
        ("k", qw + head * DK, DK),
        ("v", 2 * qw + head * DV, DV),
    ):
        offset = pl.multiple_of(offset, LANES)
        raw = read_rows(sent_ref, offset, width).astype(F32)
        taps = taps_ref[:, pl.ds(offset, width)]
        out[name] = (offset, raw, taps) + conv_silu(raw, taps, place, start)
    offset = 2 * qw + heads * DV
    pairs = read_rows(sent_ref, offset, LANES).astype(F32)
    lanes = lax.broadcasted_iota(jnp.int32, pairs.shape, 1)
    decay_in = column(pairs, lanes, 2 * head) + rate_ref[1, head]
    soft = jnp.maximum(decay_in, 0.0) + jnp.log1p(jnp.exp(-jnp.abs(decay_in)))
    out["log"] = rate_ref[0, head] * soft
    out["decay_in"] = decay_in
    out["beta"] = sigmoid(column(pairs, lanes, 2 * head + 1))
    out["lanes"] = lanes
    return out


def mixer_forward_kernel(
    micro, per_step, heads, docs, lengths_ref, rate_ref, sent_ref, taps_ref,
    mixed_ref, update_ref, inverse_ref,
):
    count = sent_ref.shape[0] * sent_ref.shape[2]
    place, start, rows, cols = pack_masks(pack_ends(lengths_ref, micro, docs), count)
    blocks = count // BLOCK
    for local in range(per_step):
        head = pl.program_id(0) * per_step + local
        made = head_inputs(sent_ref, taps_ref, rate_ref, head, heads, place, start)
        query = unit_rows(made["q"][5])[0] * DK ** (-0.5)
        keys = unit_rows(made["k"][5])[0]
        values = made["v"][5]
        beta = made["beta"]
        decay = decay_grid(made["log"], start, rows, cols)
        system = jnp.where(cols < rows, decay, 0.0) * beta * dot3(keys, keys, NT)
        target = beta * values
        updates = []
        for block in range(blocks):
            at = slice(block * BLOCK, (block + 1) * BLOCK)
            inverse = unit_lower_inverse(system[at, at])
            inverse_ref[local, block] = inverse
            right = target[at]
            for earlier in range(block):
                right = right - dot3(
                    system[at, earlier * BLOCK : (earlier + 1) * BLOCK], updates[earlier]
                )
            updates.append(dot3(inverse, right))
        update = jnp.concatenate(updates, axis=0)
        update_ref[local] = update
        scores = decay * dot1(query, keys, NT)
        write_rows(mixed_ref, pl.multiple_of(head * DV, LANES), dot1(scores, update))


def mixer_backward_kernel(
    micro, per_step, heads, docs, lengths_ref, rate_ref, sent_ref, taps_ref,
    update_ref, inverse_ref, grad_ref,
    grad_sent_ref, grad_taps_ref, small_ref,
):
    count = sent_ref.shape[0] * sent_ref.shape[2]
    place, start, rows, cols = pack_masks(pack_ends(lengths_ref, micro, docs), count)
    blocks = count // BLOCK
    pair_offset = 2 * heads * DK + heads * DV

    @pl.when(pl.program_id(0) == 0)
    def _():
        small_ref[...] = jnp.zeros_like(small_ref)
        grad_taps_ref[...] = jnp.zeros_like(grad_taps_ref)
        write_rows(grad_sent_ref, pair_offset, jnp.zeros((count, LANES), BF16))

    grad_pairs = read_rows(grad_sent_ref, pair_offset, LANES).astype(F32)
    small_lanes = lax.broadcasted_iota(jnp.int32, (1, LANES), 1)
    for local in range(per_step):
        head = pl.program_id(0) * per_step + local
        made = head_inputs(sent_ref, taps_ref, rate_ref, head, heads, place, start)
        unit_q, scale_q = unit_rows(made["q"][5])
        query = unit_q * DK ** (-0.5)
        keys, scale_k = unit_rows(made["k"][5])
        values = made["v"][5]
        beta = made["beta"]
        grad_mixed = read_rows(grad_ref, pl.multiple_of(head * DV, LANES), DV)
        decay = decay_grid(made["log"], start, rows, cols)
        strict = jnp.where(cols < rows, decay, 0.0)
        keys_keys = dot3(keys, keys, NT)
        weighted = strict * beta
        system = weighted * keys_keys
        scores = decay * dot1(query, keys, NT)
        update = update_ref[local]
        grad_scores = dot1(grad_mixed, update, NT)
        grad_update = dot1(scores, grad_mixed, TN)
        grad_targets = [None] * blocks
        for block in reversed(range(blocks)):
            at = slice(block * BLOCK, (block + 1) * BLOCK)
            right = grad_update[at]
            for later in range(block + 1, blocks):
                right = right - dot3(
                    system[later * BLOCK : (later + 1) * BLOCK, at], grad_targets[later], TN
                )
            grad_targets[block] = dot3(inverse_ref[local, block], right, TN)
        grad_target = jnp.concatenate(grad_targets, axis=0)
        grad_system = -dot1(grad_target, update, NT)
        grad_values = beta * grad_target
        grad_beta = jnp.sum(grad_target * values, axis=1, keepdims=True) + jnp.sum(
            grad_system * strict * keys_keys, axis=1, keepdims=True
        )
        grad_kk = grad_system * weighted
        grad_qk = grad_scores * decay
        grad_query = dot1(grad_qk, keys) * DK ** (-0.5)
        grad_keys = dot1(grad_kk, keys) + dot1(grad_kk, keys, TN) + dot1(grad_qk, query, TN)
        grad_spread = grad_scores * scores + grad_system * system
        lower = jnp.where(cols <= rows, 1.0, 0.0).astype(BF16)
        high, low = halves(grad_spread)
        dot = partial(lax.dot_general, dimension_numbers=TN, preferred_element_type=F32)
        after = dot(lower, high) + dot(lower, low)
        grad_log = jnp.sum(jnp.where(cols < rows, after, 0.0), axis=1, keepdims=True)
        grad_decay = grad_log * rate_ref[0, head] * sigmoid(made["decay_in"])
        grad_beta_in = grad_beta * beta * (1.0 - beta)
        lanes = made["lanes"]
        grad_pairs = jnp.where(lanes == 2 * head, grad_decay, grad_pairs)
        grad_pairs = jnp.where(lanes == 2 * head + 1, grad_beta_in, grad_pairs)
        grad_alog = jnp.sum(grad_log * made["log"], axis=0, keepdims=True)
        grad_dt = jnp.sum(grad_decay, axis=0, keepdims=True)
        small_ref[0:1] += jnp.where(small_lanes == head, grad_alog, 0.0)
        small_ref[1:2] += jnp.where(small_lanes == head, grad_dt, 0.0)
        for name, grad in (
            ("q", unit_rows_back(grad_query, made["q"][5], scale_q)),
            ("k", unit_rows_back(grad_keys, made["k"][5], scale_k)),
            ("v", grad_values),
        ):
            where, raw, taps, total, opened, _ = made[name]
            grad_raw, grad_taps = conv_silu_back(grad, total, opened, raw, taps, place, start)
            write_rows(grad_sent_ref, where, grad_raw)
            for tap in range(CONV):
                grad_taps_ref[tap : tap + 1, pl.ds(where, raw.shape[1])] += grad_taps[tap]
    write_rows(grad_sent_ref, pair_offset, grad_pairs)


def gate_forward_kernel(heads, mixed_ref, gate_ref, gain_ref, normed_ref):
    for head in range(heads):
        offset = head * DV
        mixed = read_rows(mixed_ref, offset, DV).astype(F32)
        gate = read_rows(gate_ref, offset, DV)
        scale = lax.rsqrt(jnp.mean(mixed * mixed, axis=1, keepdims=True) + EPS)
        write_rows(normed_ref, offset, mixed * scale * gain_ref[...] * (gate * sigmoid(gate)))


def gate_backward_kernel(
    heads, mixed_ref, gate_ref, gain_ref, grad_ref, grad_mixed_ref, grad_gate_ref, grad_gain_ref
):
    @pl.when(pl.program_id(0) == 0)
    def _():
        grad_gain_ref[...] = jnp.zeros_like(grad_gain_ref)

    gain = gain_ref[...]
    for head in range(heads):
        offset = head * DV
        mixed = read_rows(mixed_ref, offset, DV).astype(F32)
        gate = read_rows(gate_ref, offset, DV)
        grad = read_rows(grad_ref, offset, DV)
        scale = lax.rsqrt(jnp.mean(mixed * mixed, axis=1, keepdims=True) + EPS)
        soft = sigmoid(gate)
        plain_rows = mixed * scale
        write_rows(
            grad_gate_ref, offset, grad * plain_rows * gain * soft * (1.0 + gate * (1.0 - soft))
        )
        grad = grad * (gate * soft)
        grad_gain_ref[...] += jnp.sum(grad * plain_rows, axis=0, keepdims=True)
        grad = grad * gain
        inner = jnp.mean(mixed * grad, axis=1, keepdims=True)
        write_rows(
            grad_mixed_ref, offset, scale * grad - mixed * (scale * scale * scale * inner)
        )


def row_spec(array, micro):
    spans, micros, length, width = array.shape
    pick = micro if micros > 1 else 0
    return pl.BlockSpec((spans, 1, length, width), lambda h: (0, pick, 0, 0))


def span_spec(array, micro):
    _, micros, length, width = array.shape
    pick = micro if micros > 1 else 0
    return pl.BlockSpec((1, 1, length, width), lambda s: (s, pick, 0, 0))


def whole_spec(*dims):
    return pl.BlockSpec(dims, lambda h: (0,) * len(dims))


def mixer_cost(sent, heads, passes):
    count = sent.shape[0] * sent.shape[2]
    return pl.CostEstimate(
        flops=passes * heads * 2 * count * count * DV,
        bytes_accessed=passes * heads * count * count * 4,
        transcendentals=heads * count * count,
    )


def mixer_forward(micro, lengths, rates, sent, taps, heads):
    spans, _, length, width = sent.shape
    count, per_step = spans * length, 2 if heads % 2 == 0 else 1
    blocks = count // BLOCK
    smem = pl.BlockSpec(memory_space=pltpu.SMEM)
    mixed = jax.ShapeDtypeStruct((spans, 1, length, heads * DV), BF16)
    return pl.pallas_call(
        partial(mixer_forward_kernel, micro, per_step, heads, lengths.shape[1]),
        grid=(heads // per_step,),
        in_specs=[smem, smem, row_spec(sent, micro), whole_spec(CONV, width)],
        out_specs=[
            row_spec(mixed, 0),
            pl.BlockSpec((per_step, count, DV), lambda h: (h, 0, 0)),
            pl.BlockSpec((per_step, blocks, BLOCK, BLOCK), lambda h: (h, 0, 0, 0)),
        ],
        out_shape=[
            mixed,
            jax.ShapeDtypeStruct((heads, count, DV), F32),
            jax.ShapeDtypeStruct((heads, blocks, BLOCK, BLOCK), F32),
        ],
        compiler_params=pltpu.CompilerParams(vmem_limit_bytes=40 * 1024 * 1024),
        cost_estimate=mixer_cost(sent, heads, 60),
        name="mixer_forward",
    )(lengths, rates, sent, taps)


def mixer_backward(micro, lengths, rates, sent, taps, update, inverse, grad, heads):
    spans, _, length, width = sent.shape
    count, per_step = spans * length, 2 if heads % 2 == 0 else 1
    blocks = count // BLOCK
    smem = pl.BlockSpec(memory_space=pltpu.SMEM)
    grad_sent = jax.ShapeDtypeStruct((spans, 1, length, width), BF16)
    return pl.pallas_call(
        partial(mixer_backward_kernel, micro, per_step, heads, lengths.shape[1]),
        grid=(heads // per_step,),
        in_specs=[
            smem, smem, row_spec(sent, micro), whole_spec(CONV, width),
            pl.BlockSpec((per_step, count, DV), lambda h: (h, 0, 0)),
            pl.BlockSpec((per_step, blocks, BLOCK, BLOCK), lambda h: (h, 0, 0, 0)),
            row_spec(grad, 0),
        ],
        out_specs=[row_spec(grad_sent, 0), whole_spec(CONV, width), whole_spec(8, LANES)],
        out_shape=[
            grad_sent,
            jax.ShapeDtypeStruct((CONV, width), F32),
            jax.ShapeDtypeStruct((8, LANES), F32),
        ],
        compiler_params=pltpu.CompilerParams(vmem_limit_bytes=40 * 1024 * 1024),
        cost_estimate=mixer_cost(sent, heads, 1),
        name="mixer_backward",
    )(lengths, rates, sent, taps, update, inverse, grad)


def gate_forward(micro, mixed, gate, gain, heads):
    return pl.pallas_call(
        partial(gate_forward_kernel, heads),
        grid=(mixed.shape[0],),
        in_specs=[span_spec(mixed, 0), span_spec(gate, micro), whole_spec(1, DV)],
        out_specs=span_spec(mixed, 0),
        out_shape=jax.ShapeDtypeStruct(mixed.shape, BF16),
        cost_estimate=pl.CostEstimate(
            flops=20 * mixed.size, bytes_accessed=8 * mixed.size, transcendentals=mixed.size
        ),
        name="gate_forward",
    )(mixed, gate, gain)


def gate_backward(micro, mixed, gate, gain, grad, heads):
    out = jax.ShapeDtypeStruct(mixed.shape, BF16)
    return pl.pallas_call(
        partial(gate_backward_kernel, heads),
        grid=(mixed.shape[0],),
        in_specs=[
            span_spec(mixed, 0), span_spec(gate, micro), whole_spec(1, DV), span_spec(grad, 0),
        ],
        out_specs=[span_spec(out, 0), span_spec(out, 0), whole_spec(1, DV)],
        out_shape=[out, out, jax.ShapeDtypeStruct((1, DV), F32)],
        cost_estimate=pl.CostEstimate(
            flops=40 * mixed.size, bytes_accessed=14 * mixed.size, transcendentals=mixed.size
        ),
        name="gate_backward",
    )(mixed, gate, gain, grad)


def norm_forward_kernel(base_ref, terms_ref, gain_ref, middle_ref, rows_ref):
    middle = base_ref[...].astype(F32)
    for span in range(terms_ref.shape[0]):
        middle = middle + terms_ref[span].astype(F32)
    scale = lax.rsqrt(jnp.mean(middle * middle, axis=1, keepdims=True) + EPS)
    rows = (middle * scale * gain_ref[...]).astype(BF16)
    middle_ref[...] = middle
    for span in range(rows_ref.shape[0]):
        rows_ref[span] = rows


def norm_backward_kernel(
    base_ref, middle_ref, terms_ref, gain_ref, grad_ref, rows_ref, grad_gain_ref
):
    middle = middle_ref[...]
    grad = terms_ref[0].astype(F32)
    for span in range(1, terms_ref.shape[0]):
        grad = grad + terms_ref[span].astype(F32)
    scale = lax.rsqrt(jnp.mean(middle * middle, axis=1, keepdims=True) + EPS)
    grad_gain_ref[...] = jnp.sum(middle * scale * grad, axis=0, keepdims=True)
    inner = grad * gain_ref[...]
    weight = scale * scale * scale * jnp.mean(middle * inner, axis=1, keepdims=True)
    total = base_ref[...].astype(F32) + scale * inner - middle * weight
    grad_ref[...] = total
    rows = total.astype(BF16)
    for span in range(rows_ref.shape[0]):
        rows_ref[span] = rows


def norm_forward(base, terms, gain):
    return pl.pallas_call(
        norm_forward_kernel,
        out_shape=[
            jax.ShapeDtypeStruct(base.shape, F32),
            jax.ShapeDtypeStruct(terms.shape, BF16),
        ],
        cost_estimate=pl.CostEstimate(
            flops=20 * base.size, bytes_accessed=40 * base.size, transcendentals=0
        ),
        name="norm_forward",
    )(base, terms, gain)


def norm_backward(base, middle, terms, gain):
    return pl.pallas_call(
        norm_backward_kernel,
        out_shape=[
            jax.ShapeDtypeStruct(base.shape, F32),
            jax.ShapeDtypeStruct(terms.shape, BF16),
            jax.ShapeDtypeStruct(gain.shape, F32),
        ],
        cost_estimate=pl.CostEstimate(
            flops=30 * base.size, bytes_accessed=40 * base.size, transcendentals=0
        ),
        name="norm_backward",
    )(base, middle, terms, gain)


def dot(left, right):
    return jnp.dot(left, right, preferred_element_type=F32)


def outer(left, right):
    return lax.dot_general(left, right, TN, preferred_element_type=F32)


def dot_back(left, right):
    return lax.dot_general(left, right, NT, preferred_element_type=F32)


def after(value, *earlier):
    return lax.optimization_barrier((value,) + earlier)[0]


def plain(array):
    return with_layout_constraint(array, Layout(major_to_minor=tuple(range(array.ndim))))


def exchange(blocks):
    return lax.all_to_all(blocks, "seq", split_axis=0, concat_axis=0, tiled=True)


def gather_rows(rows):
    spans = lax.axis_size("seq")
    return exchange(jnp.broadcast_to(rows[None], (spans,) + rows.shape))


def scatter_rows(partial_rows, spans):
    return exchange(
        partial_rows.astype(BF16).reshape((spans, -1) + partial_rows.shape[1:])
    )


def cut(array, start, size, axis=0):
    return lax.dynamic_slice_in_dim(array, start, size, axis, allow_negative_indices=False)


def norm_scale(values):
    return lax.rsqrt(jnp.mean(values * values, axis=-1, keepdims=True) + EPS)


def norm_back(values, gain, grad):
    scale = norm_scale(values)
    inner = gain * grad
    back = scale * inner - values * (
        scale * scale * scale * jnp.mean(values * inner, axis=-1, keepdims=True)
    )
    return back, jnp.sum(values * scale * grad, axis=0)


def shards(
    tokens, lengths, in_weight, decay_weight, conv_weight, a_log, dt_bias, norm_gains, out_gain,
    out_weight, up_weight, down_weight, cotangent,
):
    spans, packs = lax.axis_size("seq"), lax.axis_size("fsdp")
    place = lax.axis_index("seq")
    micros, _, length, _ = tokens.shape
    heads = H // spans
    qw, vw, fw = heads * DK, heads * DV, FF // spans
    fp = round_up(fw, LANES)
    share = in_weight.shape[0]
    local_rows = micros * length

    def columns(array, start, count):
        return array[:, start : start + count * spans].reshape(share, spans, count)

    def widen(array, count):
        return jnp.pad(array, ((0, 0), (0, 0), (0, count - array.shape[2])))

    def by_span(pieces):
        return jnp.concatenate(pieces, axis=2).swapaxes(0, 1)

    def gather_weight(blocks):
        full = plain(lax.all_gather(plain(blocks), "fsdp", axis=1, tiled=True))
        return full.reshape(D, blocks.shape[2])

    conv_share = conv_weight.shape[0]
    conv_cols = CONV * conv_share // share
    small = jnp.concatenate([conv_weight.reshape(share, conv_cols), norm_gains.T], axis=1)
    small = jnp.broadcast_to(small[:, None], (share, spans, conv_cols + 2))
    pairs = jnp.concatenate([decay_weight.reshape(share, spans, 2 * heads), small], axis=2)
    pair_at = 2 * qw + vw
    mix_width = pair_at + LANES
    in_blocks = by_span([
        columns(in_weight, 0, qw),
        columns(in_weight, H * DK, qw),
        columns(in_weight, 2 * H * DK, vw),
        widen(pairs, LANES),
        columns(in_weight, 2 * H * DK + H * DV, vw),
    ])
    up_blocks = by_span([
        widen(columns(up_weight, 0, fw), fp),
        widen(columns(up_weight, FF, fw), fp),
    ])
    local_tokens = tokens.reshape(local_rows, D)
    local_cot = cotangent.reshape(local_rows, D)
    grouped = (spans, micros, length)
    all_rows = spans * local_rows

    in_blocks, up_blocks = lax.optimization_barrier((exchange(in_blocks), up_blocks))
    w_mix = gather_weight(in_blocks[:, :, :mix_width])
    all_tokens = gather_rows(after(local_tokens, in_blocks))

    cot = gather_rows(after(local_cot, all_tokens)).reshape(all_rows, D)
    small_at = pair_at + 2 * heads
    small = plain(w_mix[:, small_at : small_at + conv_cols + 2])
    gains = small[:, conv_cols:].T.astype(F32)

    def own(base, width):
        step = conv_share // share
        rows = cut(small[:, :conv_cols], base // step + place * (width // step), width // step)
        return rows.reshape(width, CONV).T

    taps = jnp.concatenate(
        [own(0, qw), own(H * DK, qw), own(2 * H * DK, vw), jnp.zeros((CONV, LANES), BF16)],
        axis=1,
    ).astype(F32)
    rates = jnp.stack([
        -jnp.exp(cut(a_log, place * heads, heads)),
        cut(dt_bias, place * heads, heads),
    ])
    gain_row = out_gain.reshape(1, DV)
    pack_lengths = lengths[:, 0]

    inputs = all_tokens.reshape(all_rows, D).astype(F32)
    input_scale = norm_scale(inputs)
    first = (inputs * input_scale * gains[0]).astype(BF16)
    sent = dot(first, w_mix).astype(BF16)
    w_gate = gather_weight(after(in_blocks, all_tokens)[:, :, mix_width:])
    w_down = lax.all_gather(after(down_weight, w_mix), "fsdp", axis=0)
    w_out = lax.all_gather(after(out_weight, w_mix), "fsdp", axis=0, tiled=True)
    sent = sent.reshape(grouped + (mix_width,))
    mixers = []
    for micro in range(micros):
        mixers.append(
            mixer_forward(micro, pack_lengths, rates, sent, taps, heads)
        )
        sent = after(sent, mixers[-1][0])
    up_blocks = exchange(after(up_blocks, cot, mixers[0][0]))
    w_down = lax.optimization_barrier(w_down.reshape(fw, D))
    gate = dot(first, w_gate).reshape(grouped + (vw,))
    grad_act = dot_back(cot, w_down).reshape(grouped + (fw,))

    def part(array, micro):
        return array.reshape((micros, length) + array.shape[1:])[micro]

    normeds, branches, branch_rows = [], [], []
    for micro in range(micros):
        normeds.append(gate_forward(micro, mixers[micro][0], gate, gain_row, heads))
        rows = dot(normeds[-1].reshape(-1, vw), w_out).astype(BF16)
        branches.append(scatter_rows(after(rows, up_blocks), spans))
        branch_rows.append(rows)
    w_up = gather_weight(after(up_blocks, branch_rows[0]))
    middles, seconds = [], []
    for micro in range(micros):
        middle, rows = norm_forward(part(local_tokens, micro), branches[micro], gains[1:])
        middles.append(middle)
        seconds.append(exchange(rows))

    acts, grad_boths, grad_seconds, sums = [], [], [], []
    for micro in range(micros):
        seconds[micro] = after(seconds[micro], *sums)
        both = dot(seconds[micro].reshape(-1, D), w_up)
        gated, upper = both[:, :fp], both[:, fp:]
        soft = jax.nn.sigmoid(gated)
        acts.append((gated * soft * upper).astype(BF16).reshape(spans, length, fp))
        grad = jnp.pad(grad_act[:, micro].reshape(-1, fw), ((0, 0), (0, fp - fw)))
        grad_both = jnp.concatenate(
            [
                (grad * upper * soft * (1.0 + gated * (1.0 - soft))).astype(BF16),
                (grad * gated * soft).astype(BF16),
            ],
            axis=1,
        )
        grad_boths.append(grad_both.reshape(spans, length, 2 * fp))
        rows = dot_back(grad_both, w_up).astype(BF16)
        grad_seconds.append(scatter_rows(rows, spans))
        sums.append(rows)
    act = jnp.stack(acts, axis=1).reshape(all_rows, fp)[:, :fw]
    final_rows = [dot(a.reshape(-1, fp)[:, :fw], w_down).astype(BF16) for a in acts]
    down_grads = outer(act, cot).astype(BF16).reshape(packs, -1, D)
    spare = [final_rows[:1], final_rows[1:] + [down_grads]]
    grad_middles, grad_branches, grad_gain2 = [], [], 0.0
    for micro in range(micros):
        terms = after(grad_seconds[micro], *spare[min(micro, 1)])
        grad_middle, rows, grad_gain = norm_backward(
            part(local_cot, micro), middles[micro], terms, gains[1:]
        )
        grad_gain2 = grad_gain2 + grad_gain
        grad_middles.append(grad_middle)
        grad_branches.append(exchange(rows))

    def reduce_rows(grad, blocks):
        blocks = plain(grad.astype(BF16).reshape(blocks, -1, grad.shape[1]))
        return plain(lax.psum_scatter(blocks, "fsdp", scatter_dimension=1, tiled=True))

    def joined(blocks, start, width):
        return blocks[:, :, start : start + width].swapaxes(0, 1).astype(F32).reshape(share, -1)

    def all_micros(parts):
        return jnp.stack(parts, axis=1).reshape(all_rows, parts[0].shape[-1])

    up_product = outer(
        after(all_micros(seconds), grad_seconds[0], *sums), all_micros(grad_boths)
    ).astype(BF16)
    up_grads = reduce_rows(up_product, spans)
    grad_gates, grad_sents, grad_gain, grad_taps, grad_small = [], [], 0.0, 0.0, 0.0
    for micro in range(micros):
        mixed, update, inverse = mixers[micro]
        grad = after(grad_branches[micro], *grad_sents)
        grad = dot_back(grad.reshape(-1, D), w_out).reshape(spans, 1, length, vw)
        grad_mixed, grad_gate, term = gate_backward(micro, mixed, gate, gain_row, grad, heads)
        if micro + 1 == micros:
            grad_mixed = after(grad_mixed, up_grads)
        grad_sent, term_taps, term_small = mixer_backward(
            micro, pack_lengths, rates, sent, taps, update, inverse, grad_mixed, heads
        )
        grad_gates.append(grad_gate.reshape(spans, length, vw))
        grad_sents.append(grad_sent.reshape(spans, length, mix_width))
        grad_gain, grad_taps = grad_gain + term, grad_taps + term_taps
        grad_small = grad_small + term_small
    finals, wait = [], grad_sents[0]
    for micro in range(micros):
        wait = scatter_rows(after(final_rows[micro], wait), spans)
        finals.append(wait)
    block_out = jnp.stack([
        middle + jnp.sum(terms.astype(F32), axis=0) for middle, terms in zip(middles, finals)
    ]).reshape(local_rows, D)

    grad_proj = all_micros([
        jnp.concatenate(pair, axis=-1) for pair in zip(grad_sents, grad_gates)
    ])
    grad_down = lax.psum_scatter(
        after(down_grads, grad_middles[0]), "fsdp", scatter_dimension=0
    )
    in_product = outer(after(first, finals[0]), grad_proj)
    in_grads = reduce_rows(in_product, spans)
    grad_proj = after(grad_proj, in_product, finals[-1])
    grad_first = dot_back(grad_proj[:, :mix_width], w_mix) + dot_back(
        grad_proj[:, mix_width:], w_gate
    )
    grad_gain1 = jnp.sum(inputs * input_scale * grad_first, axis=0)
    first_rows = grad_first.astype(BF16)
    first_rows, grad_down, up_grads = lax.optimization_barrier((first_rows, grad_down, up_grads))
    grad_first = scatter_rows(first_rows, spans)
    out_grads = outer(
        all_micros([n[:, 0] for n in normeds]), after(all_micros(grad_branches), first_rows)
    )
    grad_out = lax.psum_scatter(
        out_grads.astype(BF16), "fsdp", scatter_dimension=0, tiled=True
    ).astype(F32)
    grad_norm1, _ = norm_back(
        local_tokens.astype(F32), gains[0], jnp.sum(grad_first.astype(F32), axis=0)
    )
    grad_tokens = jnp.stack(grad_middles).reshape(local_rows, D) + grad_norm1
    up_grads = exchange(after(up_grads, grad_first))
    in_grads = exchange(after(in_grads, up_grads))
    grad_up = jnp.concatenate([joined(up_grads, 0, fw), joined(up_grads, fp, fw)], axis=1)
    grad_in = jnp.concatenate(
        [
            joined(in_grads, 0, qw),
            joined(in_grads, qw, qw),
            joined(in_grads, 2 * qw, vw),
            joined(in_grads, mix_width, vw),
        ],
        axis=1,
    )
    grad_decay = joined(in_grads, pair_at, 2 * heads)

    gain_rows = jnp.stack([grad_gain1, grad_gain2[0]])
    flat = jnp.concatenate([
        grad_taps[:, :pair_at].reshape(-1), gain_rows.reshape(-1), grad_gain.reshape(-1),
        grad_small[:2].reshape(-1),
    ])
    flat = jnp.pad(flat, (0, round_up(flat.size, 8 * LANES) - flat.size)).reshape(-1, LANES)
    flat = lax.psum(flat, "fsdp")
    flat = lax.all_gather(flat, "seq", axis=0).reshape(spans, -1)
    taps_flat = flat[:, : CONV * pair_at].reshape(spans, CONV, pair_at)

    def all_taps(start, width):
        return taps_flat[:, :, start : start + width].swapaxes(0, 1).reshape(CONV, -1)

    grad_conv = jnp.concatenate(
        [all_taps(0, qw), all_taps(qw, qw), all_taps(2 * qw, vw)], axis=1
    )
    index = place * packs + lax.axis_index("fsdp")
    grad_conv = cut(grad_conv, index * conv_share, conv_share, 1).T
    at = CONV * pair_at
    gains_flat = jnp.sum(flat[:, at : at + 2 * D], axis=0).reshape(2, D)
    gain_share = norm_gains.shape[1]
    grad_gains = cut(gains_flat, index * gain_share, gain_share, 1)
    at = at + 2 * D
    grad_gain = jnp.sum(flat[:, at : at + DV], axis=0)
    at = at + DV
    return (
        block_out.astype(BF16).reshape(micros, 1, length, D),
        grad_tokens.reshape(micros, 1, length, D),
        grad_in,
        grad_decay,
        grad_conv,
        flat[:, at : at + heads].reshape(H),
        flat[:, at + LANES : at + LANES + heads].reshape(H),
        grad_gains,
        grad_gain,
        grad_out,
        grad_up,
        grad_down.astype(F32),
    )


def solution(mesh):
    rows = P(("seq", "fsdp"), None)
    packs = P(None, "fsdp", "seq", None)
    gains = P(None, ("seq", "fsdp"))
    return jax.shard_map(
        shards,
        mesh=mesh,
        in_specs=(
            packs, P(None, "fsdp", None), rows, rows, rows, P(), P(), gains, P(), rows, rows, rows,
            packs,
        ),
        out_specs=(packs, packs, rows, rows, rows, P(), P(), gains, P(), rows, rows, rows),
        check_vma=False,
    )
```

```python
from functools import partial

import jax
import jax.numpy as jnp
from jax import lax
from jax.experimental import pallas as pl
from jax.experimental.layout import Layout, with_layout_constraint
from jax.experimental.pallas import tpu as pltpu
from jax.sharding import PartitionSpec as P

D = 2048
H = 16
DK = 128
DV = 256
FF = 5504
CONV = 4
EPS = 1e-06
BLOCK = 128
LANES = 128
F32 = jnp.float32
BF16 = jnp.bfloat16


def round_up(value, step):
    return -(-value // step) * step


NN = (((1,), (0,)), ((), ()))
NT = (((1,), (1,)), ((), ()))
TN = (((0,), (0,)), ((), ()))


def dot1(left, right, form=NN):
    return lax.dot_general(
        left.astype(BF16), right.astype(BF16), form, preferred_element_type=F32
    )


def halves(value):
    high = value.astype(BF16)
    return high, (value - high.astype(F32)).astype(BF16)


def dot3(left, right, form=NN):
    left_high, left_low = halves(left)
    right_high, right_low = halves(right)
    dot = partial(lax.dot_general, dimension_numbers=form, preferred_element_type=F32)
    return dot(left_high, right_high) + (dot(left_high, right_low) + dot(left_low, right_high))


def sigmoid(value):
    return 1.0 / (1.0 + jnp.exp(-value))


def pack_masks(ends, count):
    place = lax.broadcasted_iota(jnp.int32, (count, 1), 0)
    start = jnp.zeros((count, 1), jnp.int32)
    for end in ends:
        start = jnp.where(place >= end, jnp.maximum(start, end), start)
    rows = lax.broadcasted_iota(jnp.int32, (count, count), 0)
    cols = lax.broadcasted_iota(jnp.int32, (count, count), 1)
    return place, start, rows, cols


def conv_silu(raw, taps, place, start):
    total = raw * taps[CONV - 1 : CONV]
    for lag in range(1, CONV):
        moved = pltpu.roll(raw, lag, 0)
        same = place - lag >= start
        total = total + jnp.where(same, moved, 0.0) * taps[CONV - 1 - lag : CONV - lag]
    gate = sigmoid(total)
    return total, gate, total * gate


def conv_silu_back(grad, total, gate, raw, taps, place, start):
    grad_total = grad * gate * (1.0 + total * (1.0 - gate))
    grad_raw = grad_total * taps[CONV - 1 : CONV]
    grad_taps = [None] * CONV
    grad_taps[CONV - 1] = jnp.sum(grad_total * raw, axis=0, keepdims=True)
    count = raw.shape[0]
    for lag in range(1, CONV):
        same = place - lag >= start
        kept = jnp.where(same, grad_total, 0.0)
        moved = pltpu.roll(raw, lag, 0)
        grad_taps[CONV - 1 - lag] = jnp.sum(kept * moved, axis=0, keepdims=True)
        grad_raw = grad_raw + pltpu.roll(kept, count - lag, 0) * taps[CONV - 1 - lag : CONV - lag]
    return grad_raw, grad_taps


def unit_rows(values):
    scale = lax.rsqrt(jnp.sum(values * values, axis=1, keepdims=True) + EPS)
    return values * scale, scale


def unit_rows_back(grad, values, scale):
    inner = jnp.sum(values * grad, axis=1, keepdims=True)
    return scale * grad - values * (scale * scale * scale * inner)


def column(values, lanes, index):
    return jnp.sum(jnp.where(lanes == index, values, 0.0), axis=1, keepdims=True)


def decay_grid(log_rate, start, rows, cols):
    count = log_rate.shape[0]
    lower = jnp.where(cols <= rows, 1.0, 0.0).astype(BF16)
    spread = jnp.where(cols < rows, jnp.broadcast_to(log_rate, (count, count)), 0.0)
    first = spread.astype(BF16)
    rest = spread - first.astype(F32)
    second = rest.astype(BF16)
    third = (rest - second.astype(F32)).astype(BF16)
    dot = partial(lax.dot_general, dimension_numbers=NN, preferred_element_type=F32)
    summed = dot(lower, first) + (dot(lower, second) + dot(lower, third))
    inside = (cols <= rows) & (cols >= start)
    return jnp.where(inside, jnp.exp(jnp.where(inside, summed, 0.0)), 0.0)


def unit_lower_inverses(blocks):
    size = blocks[0].shape[0]
    rows = lax.broadcasted_iota(jnp.int32, (size, size), 0)
    cols = lax.broadcasted_iota(jnp.int32, (size, size), 1)
    level, results = 0, []
    while (1 << level) < size:
        width = 1 << level
        joint = (
            ((rows >> (level + 1)) == (cols >> (level + 1)))
            & ((rows & width) != 0)
            & ((cols & width) == 0)
        )
        parts = [jnp.where(joint, block, 0.0) for block in blocks]
        if level == 0:
            unit = jnp.where(rows == cols, 1.0, 0.0).astype(F32)
            results = [unit - part for part in parts]
        else:
            inner = [dot3(part, result) for part, result in zip(parts, results)]
            results = [result - dot3(result, term) for result, term in zip(results, inner)]
        level += 1
    return results


def read_rows(ref, offset, width):
    shape = ref.shape
    return ref[:, 0, :, pl.ds(offset, width)].reshape(shape[0] * shape[2], width)


def write_rows(ref, offset, value):
    shape = ref.shape
    ref[:, 0, :, pl.ds(offset, value.shape[1])] = value.reshape(
        shape[0], shape[2], value.shape[1]
    ).astype(ref.dtype)


def pack_ends(lengths_ref, micro, docs):
    ends, total = [], 0
    for index in range(docs - 1):
        total = total + lengths_ref[micro, index]
        ends.append(total)
    return ends


def head_inputs(sent_ref, taps_ref, rate_ref, head, heads, place, start):
    qw = heads * DK
    out = {}
    for name, offset, width in (
        ("q", head * DK, DK),
        ("k", qw + head * DK, DK),
        ("v", 2 * qw + head * DV, DV),
    ):
        offset = pl.multiple_of(offset, LANES)
        raw = read_rows(sent_ref, offset, width).astype(F32)
        taps = taps_ref[:, pl.ds(offset, width)]
        out[name] = (offset, raw, taps) + conv_silu(raw, taps, place, start)
    offset = 2 * qw + heads * DV
    pairs = read_rows(sent_ref, offset, LANES).astype(F32)
    lanes = lax.broadcasted_iota(jnp.int32, pairs.shape, 1)
    decay_in = column(pairs, lanes, 2 * head) + rate_ref[1, head]
    soft = jnp.maximum(decay_in, 0.0) + jnp.log1p(jnp.exp(-jnp.abs(decay_in)))
    out["log"] = rate_ref[0, head] * soft
    out["decay_in"] = decay_in
    out["beta"] = sigmoid(column(pairs, lanes, 2 * head + 1))
    out["lanes"] = lanes
    return out


def mixer_forward_kernel(
    micro, per_step, heads, docs, lengths_ref, rate_ref, sent_ref, taps_ref,
    mixed_ref, update_ref, inverse_ref,
):
    count = sent_ref.shape[0] * sent_ref.shape[2]
    place, start, rows, cols = pack_masks(pack_ends(lengths_ref, micro, docs), count)
    blocks = count // BLOCK
    parts = []
    for local in range(per_step):
        head = pl.program_id(0) * per_step + local
        made = head_inputs(sent_ref, taps_ref, rate_ref, head, heads, place, start)
        query = unit_rows(made["q"][5])[0] * DK ** (-0.5)
        keys = unit_rows(made["k"][5])[0]
        beta = made["beta"]
        decay = decay_grid(made["log"], start, rows, cols)
        system = jnp.where(cols < rows, decay, 0.0) * beta * dot3(keys, keys, NT)
        parts.append((system, beta * made["v"][5], decay * dot1(query, keys, NT)))
    spans = [slice(block * BLOCK, (block + 1) * BLOCK) for block in range(blocks)]
    inverses = unit_lower_inverses([system[at, at] for system, _, _ in parts for at in spans])
    for local in range(per_step):
        system, target, scores = parts[local]
        updates = []
        for block, at in enumerate(spans):
            inverse = inverses[local * blocks + block]
            inverse_ref[local, block] = inverse
            right = target[at]
            for earlier in range(block):
                right = right - dot3(system[at, spans[earlier]], updates[earlier])
            updates.append(dot3(inverse, right))
        update = jnp.concatenate(updates, axis=0)
        update_ref[local] = update
        head = pl.program_id(0) * per_step + local
        write_rows(mixed_ref, pl.multiple_of(head * DV, LANES), dot1(scores, update))


def mixer_backward_kernel(
    micro, per_step, heads, docs, lengths_ref, rate_ref, sent_ref, taps_ref,
    update_ref, inverse_ref, grad_ref,
    grad_sent_ref, grad_taps_ref, small_ref,
):
    count = sent_ref.shape[0] * sent_ref.shape[2]
    place, start, rows, cols = pack_masks(pack_ends(lengths_ref, micro, docs), count)
    blocks = count // BLOCK
    pair_offset = 2 * heads * DK + heads * DV

    @pl.when(pl.program_id(0) == 0)
    def _():
        small_ref[...] = jnp.zeros_like(small_ref)
        grad_taps_ref[...] = jnp.zeros_like(grad_taps_ref)
        write_rows(grad_sent_ref, pair_offset, jnp.zeros((count, LANES), BF16))

    grad_pairs = read_rows(grad_sent_ref, pair_offset, LANES).astype(F32)
    small_lanes = lax.broadcasted_iota(jnp.int32, (1, LANES), 1)
    for local in range(per_step):
        head = pl.program_id(0) * per_step + local
        made = head_inputs(sent_ref, taps_ref, rate_ref, head, heads, place, start)
        unit_q, scale_q = unit_rows(made["q"][5])
        query = unit_q * DK ** (-0.5)
        keys, scale_k = unit_rows(made["k"][5])
        values = made["v"][5]
        beta = made["beta"]
        grad_mixed = read_rows(grad_ref, pl.multiple_of(head * DV, LANES), DV)
        decay = decay_grid(made["log"], start, rows, cols)
        strict = jnp.where(cols < rows, decay, 0.0)
        keys_keys = dot3(keys, keys, NT)
        weighted = strict * beta
        system = weighted * keys_keys
        scores = decay * dot1(query, keys, NT)
        update = update_ref[local]
        grad_scores = dot1(grad_mixed, update, NT)
        grad_update = dot1(scores, grad_mixed, TN)
        grad_targets = [None] * blocks
        for block in reversed(range(blocks)):
            at = slice(block * BLOCK, (block + 1) * BLOCK)
            right = grad_update[at]
            for later in range(block + 1, blocks):
                right = right - dot3(
                    system[later * BLOCK : (later + 1) * BLOCK, at], grad_targets[later], TN
                )
            grad_targets[block] = dot3(inverse_ref[local, block], right, TN)
        grad_target = jnp.concatenate(grad_targets, axis=0)
        grad_system = -dot1(grad_target, update, NT)
        grad_values = beta * grad_target
        grad_beta = jnp.sum(grad_target * values, axis=1, keepdims=True) + jnp.sum(
            grad_system * strict * keys_keys, axis=1, keepdims=True
        )
        grad_kk = grad_system * weighted
        grad_qk = grad_scores * decay
        grad_query = dot1(grad_qk, keys) * DK ** (-0.5)
        grad_keys = dot1(grad_kk, keys) + dot1(grad_kk, keys, TN) + dot1(grad_qk, query, TN)
        grad_spread = grad_scores * scores + grad_system * system
        lower = jnp.where(cols <= rows, 1.0, 0.0).astype(BF16)
        high, low = halves(grad_spread)
        dot = partial(lax.dot_general, dimension_numbers=TN, preferred_element_type=F32)
        after = dot(lower, high) + dot(lower, low)
        grad_log = jnp.sum(jnp.where(cols < rows, after, 0.0), axis=1, keepdims=True)
        grad_decay = grad_log * rate_ref[0, head] * sigmoid(made["decay_in"])
        grad_beta_in = grad_beta * beta * (1.0 - beta)
        lanes = made["lanes"]
        grad_pairs = jnp.where(lanes == 2 * head, grad_decay, grad_pairs)
        grad_pairs = jnp.where(lanes == 2 * head + 1, grad_beta_in, grad_pairs)
        grad_alog = jnp.sum(grad_log * made["log"], axis=0, keepdims=True)
        grad_dt = jnp.sum(grad_decay, axis=0, keepdims=True)
        small_ref[0:1] += jnp.where(small_lanes == head, grad_alog, 0.0)
        small_ref[1:2] += jnp.where(small_lanes == head, grad_dt, 0.0)
        for name, grad in (
            ("q", unit_rows_back(grad_query, made["q"][5], scale_q)),
            ("k", unit_rows_back(grad_keys, made["k"][5], scale_k)),
            ("v", grad_values),
        ):
            where, raw, taps, total, opened, _ = made[name]
            grad_raw, grad_taps = conv_silu_back(grad, total, opened, raw, taps, place, start)
            write_rows(grad_sent_ref, where, grad_raw)
            for tap in range(CONV):
                grad_taps_ref[tap : tap + 1, pl.ds(where, raw.shape[1])] += grad_taps[tap]
    write_rows(grad_sent_ref, pair_offset, grad_pairs)


def gate_forward_kernel(heads, mixed_ref, gate_ref, gain_ref, normed_ref):
    for head in range(heads):
        offset = head * DV
        mixed = read_rows(mixed_ref, offset, DV).astype(F32)
        gate = read_rows(gate_ref, offset, DV)
        scale = lax.rsqrt(jnp.mean(mixed * mixed, axis=1, keepdims=True) + EPS)
        write_rows(normed_ref, offset, mixed * scale * gain_ref[...] * (gate * sigmoid(gate)))


def gate_backward_kernel(
    heads, mixed_ref, gate_ref, gain_ref, grad_ref, grad_mixed_ref, grad_gate_ref, grad_gain_ref
):
    @pl.when(pl.program_id(0) == 0)
    def _():
        grad_gain_ref[...] = jnp.zeros_like(grad_gain_ref)

    gain = gain_ref[...]
    for head in range(heads):
        offset = head * DV
        mixed = read_rows(mixed_ref, offset, DV).astype(F32)
        gate = read_rows(gate_ref, offset, DV)
        grad = read_rows(grad_ref, offset, DV)
        scale = lax.rsqrt(jnp.mean(mixed * mixed, axis=1, keepdims=True) + EPS)
        soft = sigmoid(gate)
        plain_rows = mixed * scale
        write_rows(
            grad_gate_ref, offset, grad * plain_rows * gain * soft * (1.0 + gate * (1.0 - soft))
        )
        grad = grad * (gate * soft)
        grad_gain_ref[...] += jnp.sum(grad * plain_rows, axis=0, keepdims=True)
        grad = grad * gain
        inner = jnp.mean(mixed * grad, axis=1, keepdims=True)
        write_rows(
            grad_mixed_ref, offset, scale * grad - mixed * (scale * scale * scale * inner)
        )


def pack_kernel(query_ref, key_ref, value_ref, pairs_ref, gate_ref, out_ref):
    at = 0
    for ref in (query_ref, key_ref, value_ref, pairs_ref, gate_ref):
        block = ref[...].reshape(out_ref.shape[1], ref.shape[-1])
        out_ref[0, :, at : at + ref.shape[-1]] = block
        at += ref.shape[-1]


def pack_columns(weight, pairs, spans):
    rows = weight.shape[0]
    qw, vw = H * DK // spans, H * DV // spans
    width = 2 * qw + 2 * vw + pairs.shape[2]
    start = 2 * H * DK // vw

    def spec(columns, first):
        return pl.BlockSpec((rows, columns), lambda s: (0, first + s))

    return pl.pallas_call(
        pack_kernel,
        grid=(spans,),
        in_specs=[
            spec(qw, 0), spec(qw, spans), spec(vw, start),
            pl.BlockSpec((1, rows, pairs.shape[2]), lambda s: (s, 0, 0)),
            spec(vw, start + spans),
        ],
        out_specs=pl.BlockSpec((1, rows, width), lambda s: (s, 0, 0)),
        out_shape=jax.ShapeDtypeStruct((spans, rows, width), BF16),
        name="pack_columns",
    )(weight, weight, weight, pairs, weight)


def row_spec(array, micro):
    spans, micros, length, width = array.shape
    pick = micro if micros > 1 else 0
    return pl.BlockSpec((spans, 1, length, width), lambda h: (0, pick, 0, 0))


def span_spec(array, micro):
    _, micros, length, width = array.shape
    pick = micro if micros > 1 else 0
    return pl.BlockSpec((1, 1, length, width), lambda s: (s, pick, 0, 0))


def whole_spec(*dims):
    return pl.BlockSpec(dims, lambda h: (0,) * len(dims))


def mixer_cost(sent, heads, passes):
    count = sent.shape[0] * sent.shape[2]
    return pl.CostEstimate(
        flops=passes * heads * 2 * count * count * DV,
        bytes_accessed=passes * heads * count * count * 4,
        transcendentals=heads * count * count,
    )


def mixer_forward(micro, lengths, rates, sent, taps, heads):
    spans, _, length, width = sent.shape
    count, per_step = spans * length, 4 if heads % 4 == 0 else 1 + (heads % 2 == 0)
    blocks = count // BLOCK
    smem = pl.BlockSpec(memory_space=pltpu.SMEM)
    mixed = jax.ShapeDtypeStruct((spans, 1, length, heads * DV), BF16)
    return pl.pallas_call(
        partial(mixer_forward_kernel, micro, per_step, heads, lengths.shape[1]),
        grid=(heads // per_step,),
        in_specs=[smem, smem, row_spec(sent, micro), whole_spec(CONV, width)],
        out_specs=[
            row_spec(mixed, 0),
            pl.BlockSpec((per_step, count, DV), lambda h: (h, 0, 0)),
            pl.BlockSpec((per_step, blocks, BLOCK, BLOCK), lambda h: (h, 0, 0, 0)),
        ],
        out_shape=[
            mixed,
            jax.ShapeDtypeStruct((heads, count, DV), F32),
            jax.ShapeDtypeStruct((heads, blocks, BLOCK, BLOCK), F32),
        ],
        compiler_params=pltpu.CompilerParams(vmem_limit_bytes=40 * 1024 * 1024),
        cost_estimate=mixer_cost(sent, heads, 60),
        name="mixer_forward",
    )(lengths, rates, sent, taps)


def mixer_backward(micro, lengths, rates, sent, taps, update, inverse, grad, heads):
    spans, _, length, width = sent.shape
    count, per_step = spans * length, 2 if heads % 2 == 0 else 1
    blocks = count // BLOCK
    smem = pl.BlockSpec(memory_space=pltpu.SMEM)
    grad_sent = jax.ShapeDtypeStruct((spans, 1, length, width), BF16)
    return pl.pallas_call(
        partial(mixer_backward_kernel, micro, per_step, heads, lengths.shape[1]),
        grid=(heads // per_step,),
        in_specs=[
            smem, smem, row_spec(sent, micro), whole_spec(CONV, width),
            pl.BlockSpec((per_step, count, DV), lambda h: (h, 0, 0)),
            pl.BlockSpec((per_step, blocks, BLOCK, BLOCK), lambda h: (h, 0, 0, 0)),
            row_spec(grad, 0),
        ],
        out_specs=[row_spec(grad_sent, 0), whole_spec(CONV, width), whole_spec(8, LANES)],
        out_shape=[
            grad_sent,
            jax.ShapeDtypeStruct((CONV, width), F32),
            jax.ShapeDtypeStruct((8, LANES), F32),
        ],
        compiler_params=pltpu.CompilerParams(vmem_limit_bytes=40 * 1024 * 1024),
        cost_estimate=mixer_cost(sent, heads, 40),
        name="mixer_backward",
    )(lengths, rates, sent, taps, update, inverse, grad)


def gate_forward(micro, mixed, gate, gain, heads):
    return pl.pallas_call(
        partial(gate_forward_kernel, heads),
        grid=(mixed.shape[0],),
        in_specs=[span_spec(mixed, 0), span_spec(gate, micro), whole_spec(1, DV)],
        out_specs=span_spec(mixed, 0),
        out_shape=jax.ShapeDtypeStruct(mixed.shape, BF16),
        cost_estimate=pl.CostEstimate(
            flops=20 * mixed.size, bytes_accessed=8 * mixed.size, transcendentals=mixed.size
        ),
        name="gate_forward",
    )(mixed, gate, gain)


def gate_backward(micro, mixed, gate, gain, grad, heads):
    out = jax.ShapeDtypeStruct(mixed.shape, BF16)
    return pl.pallas_call(
        partial(gate_backward_kernel, heads),
        grid=(mixed.shape[0],),
        in_specs=[
            span_spec(mixed, 0), span_spec(gate, micro), whole_spec(1, DV), span_spec(grad, 0),
        ],
        out_specs=[span_spec(out, 0), span_spec(out, 0), whole_spec(1, DV)],
        out_shape=[out, out, jax.ShapeDtypeStruct((1, DV), F32)],
        cost_estimate=pl.CostEstimate(
            flops=40 * mixed.size, bytes_accessed=14 * mixed.size, transcendentals=mixed.size
        ),
        name="gate_backward",
    )(mixed, gate, gain, grad)


def norm_forward_kernel(base_ref, terms_ref, gain_ref, middle_ref, rows_ref):
    middle = base_ref[...].astype(F32)
    for span in range(terms_ref.shape[0]):
        middle = middle + terms_ref[span].astype(F32)
    scale = lax.rsqrt(jnp.mean(middle * middle, axis=1, keepdims=True) + EPS)
    rows = (middle * scale * gain_ref[...]).astype(BF16)
    middle_ref[...] = middle
    for span in range(rows_ref.shape[0]):
        rows_ref[span] = rows


def norm_backward_kernel(
    base_ref, middle_ref, terms_ref, gain_ref, grad_ref, rows_ref, grad_gain_ref
):
    middle = middle_ref[...]
    grad = terms_ref[0].astype(F32)
    for span in range(1, terms_ref.shape[0]):
        grad = grad + terms_ref[span].astype(F32)
    scale = lax.rsqrt(jnp.mean(middle * middle, axis=1, keepdims=True) + EPS)
    grad_gain_ref[...] = jnp.sum(middle * scale * grad, axis=0, keepdims=True)
    inner = grad * gain_ref[...]
    weight = scale * scale * scale * jnp.mean(middle * inner, axis=1, keepdims=True)
    total = base_ref[...].astype(F32) + scale * inner - middle * weight
    grad_ref[...] = total
    rows = total.astype(BF16)
    for span in range(rows_ref.shape[0]):
        rows_ref[span] = rows


def norm_forward(base, terms, gain):
    return pl.pallas_call(
        norm_forward_kernel,
        out_shape=[
            jax.ShapeDtypeStruct(base.shape, F32),
            jax.ShapeDtypeStruct(terms.shape, BF16),
        ],
        cost_estimate=pl.CostEstimate(
            flops=20 * base.size, bytes_accessed=40 * base.size, transcendentals=0
        ),
        name="norm_forward",
    )(base, terms, gain)


def norm_backward(base, middle, terms, gain):
    return pl.pallas_call(
        norm_backward_kernel,
        out_shape=[
            jax.ShapeDtypeStruct(base.shape, F32),
            jax.ShapeDtypeStruct(terms.shape, BF16),
            jax.ShapeDtypeStruct(gain.shape, F32),
        ],
        cost_estimate=pl.CostEstimate(
            flops=30 * base.size, bytes_accessed=40 * base.size, transcendentals=0
        ),
        name="norm_backward",
    )(base, middle, terms, gain)


def dot(left, right):
    return jnp.dot(left, right, preferred_element_type=F32)


def outer(left, right):
    return lax.dot_general(left, right, TN, preferred_element_type=F32)


def dot_back(left, right):
    return lax.dot_general(left, right, NT, preferred_element_type=F32)


def after(value, *earlier):
    return lax.optimization_barrier((value,) + earlier)[0]


def plain(array):
    return with_layout_constraint(array, Layout(major_to_minor=tuple(range(array.ndim))))


def exchange(blocks):
    return lax.all_to_all(blocks, "seq", split_axis=0, concat_axis=0, tiled=True)


def gather_rows(rows):
    spans = lax.axis_size("seq")
    return exchange(jnp.broadcast_to(rows[None], (spans,) + rows.shape))


def scatter_rows(partial_rows, spans):
    return exchange(
        partial_rows.astype(BF16).reshape((spans, -1) + partial_rows.shape[1:])
    )


def cut(array, start, size, axis=0):
    return lax.dynamic_slice_in_dim(array, start, size, axis, allow_negative_indices=False)


def norm_scale(values):
    return lax.rsqrt(jnp.mean(values * values, axis=-1, keepdims=True) + EPS)


def norm_back(values, gain, grad):
    scale = norm_scale(values)
    inner = gain * grad
    back = scale * inner - values * (
        scale * scale * scale * jnp.mean(values * inner, axis=-1, keepdims=True)
    )
    return back, jnp.sum(values * scale * grad, axis=0)


def shards(
    tokens, lengths, in_weight, decay_weight, conv_weight, a_log, dt_bias, norm_gains, out_gain,
    out_weight, up_weight, down_weight, cotangent,
):
    spans, packs = lax.axis_size("seq"), lax.axis_size("fsdp")
    place = lax.axis_index("seq")
    micros, _, length, _ = tokens.shape
    heads = H // spans
    qw, vw, fw = heads * DK, heads * DV, FF // spans
    fp = round_up(fw, LANES)
    share = in_weight.shape[0]
    local_rows = micros * length

    def columns(array, start, count):
        return array[:, start : start + count * spans].reshape(share, spans, count)

    def widen(array, count):
        return jnp.pad(array, ((0, 0), (0, 0), (0, count - array.shape[2])))

    def by_span(pieces):
        return jnp.concatenate(pieces, axis=2).swapaxes(0, 1)

    def gather_weight(blocks):
        full = plain(lax.all_gather(plain(blocks), "fsdp", axis=1, tiled=True))
        return full.reshape(D, blocks.shape[2])

    conv_share = conv_weight.shape[0]
    conv_cols = CONV * conv_share // share
    small = jnp.concatenate([conv_weight.reshape(share, conv_cols), norm_gains.T], axis=1)
    small = jnp.broadcast_to(small[:, None], (share, spans, conv_cols + 2))
    pairs = jnp.concatenate([decay_weight.reshape(share, spans, 2 * heads), small], axis=2)
    pair_at = 2 * qw + vw
    mix_width = pair_at + LANES
    in_blocks = pack_columns(in_weight, widen(pairs, LANES).swapaxes(0, 1), spans)
    up_blocks = by_span([
        widen(columns(up_weight, 0, fw), fp),
        widen(columns(up_weight, FF, fw), fp),
    ])
    local_tokens = tokens.reshape(local_rows, D)
    local_cot = cotangent.reshape(local_rows, D)
    grouped = (spans, micros, length)
    all_rows = spans * local_rows

    in_blocks, up_blocks = lax.optimization_barrier((exchange(in_blocks), up_blocks))
    w_mix = gather_weight(in_blocks[:, :, :mix_width])
    all_tokens = gather_rows(after(local_tokens, in_blocks))

    cot = gather_rows(after(local_cot, all_tokens)).reshape(all_rows, D)
    small_at = pair_at + 2 * heads
    small = plain(w_mix[:, small_at : small_at + conv_cols + 2])
    gains = small[:, conv_cols:].T.astype(F32)

    def own(base, width):
        step = conv_share // share
        rows = cut(small[:, :conv_cols], base // step + place * (width // step), width // step)
        return rows.reshape(width, CONV).T

    taps = jnp.concatenate(
        [own(0, qw), own(H * DK, qw), own(2 * H * DK, vw), jnp.zeros((CONV, LANES), BF16)],
        axis=1,
    ).astype(F32)
    rates = jnp.stack([
        -jnp.exp(cut(a_log, place * heads, heads)),
        cut(dt_bias, place * heads, heads),
    ])
    gain_row = out_gain.reshape(1, DV)
    pack_lengths = lengths[:, 0]

    inputs = all_tokens.reshape(all_rows, D).astype(F32)
    input_scale = norm_scale(inputs)
    first = (inputs * input_scale * gains[0]).astype(BF16)
    sent = dot(first, w_mix).astype(BF16)
    w_gate = gather_weight(after(in_blocks, all_tokens)[:, :, mix_width:])
    w_down = lax.all_gather(after(down_weight, w_mix), "fsdp", axis=0)
    w_out = lax.all_gather(after(out_weight, w_mix), "fsdp", axis=0, tiled=True)
    sent = sent.reshape(grouped + (mix_width,))
    mixers = []
    for micro in range(micros):
        mixers.append(
            mixer_forward(micro, pack_lengths, rates, sent, taps, heads)
        )
        sent = after(sent, mixers[-1][0])
    up_blocks = exchange(after(up_blocks, cot, mixers[0][0]))
    w_down = lax.optimization_barrier(w_down.reshape(fw, D))
    gate = dot(first, w_gate).reshape(grouped + (vw,))
    grad_act = dot_back(cot, w_down).reshape(grouped + (fw,))

    def part(array, micro):
        return array.reshape((micros, length) + array.shape[1:])[micro]

    normeds, branches, branch_rows = [], [], []
    for micro in range(micros):
        normeds.append(gate_forward(micro, mixers[micro][0], gate, gain_row, heads))
        rows = dot(normeds[-1].reshape(-1, vw), w_out).astype(BF16)
        branches.append(scatter_rows(after(rows, up_blocks), spans))
        branch_rows.append(rows)
    w_up = gather_weight(after(up_blocks, branch_rows[0]))
    middles, seconds = [], []
    for micro in range(micros):
        middle, rows = norm_forward(part(local_tokens, micro), branches[micro], gains[1:])
        middles.append(middle)
        seconds.append(exchange(rows))

    acts, grad_boths, grad_seconds, sums = [], [], [], []
    for micro in range(micros):
        seconds[micro] = after(seconds[micro], *sums)
        both = dot(seconds[micro].reshape(-1, D), w_up)
        gated, upper = both[:, :fp], both[:, fp:]
        soft = jax.nn.sigmoid(gated)
        acts.append((gated * soft * upper).astype(BF16).reshape(spans, length, fp))
        grad = jnp.pad(grad_act[:, micro].reshape(-1, fw), ((0, 0), (0, fp - fw)))
        grad_both = jnp.concatenate(
            [
                (grad * upper * soft * (1.0 + gated * (1.0 - soft))).astype(BF16),
                (grad * gated * soft).astype(BF16),
            ],
            axis=1,
        )
        grad_boths.append(grad_both.reshape(spans, length, 2 * fp))
        rows = dot_back(grad_both, w_up).astype(BF16)
        grad_seconds.append(scatter_rows(rows, spans))
        sums.append(rows)
    act = jnp.stack(acts, axis=1).reshape(all_rows, fp)[:, :fw]
    final_rows = [dot(a.reshape(-1, fp)[:, :fw], w_down).astype(BF16) for a in acts]
    down_grads = outer(after(act, act), cot).astype(BF16).reshape(packs, -1, D)
    spare = [final_rows[:1], final_rows[1:] + [down_grads]]
    grad_middles, grad_branches, grad_gain2 = [], [], 0.0
    for micro in range(micros):
        terms = after(grad_seconds[micro], *spare[min(micro, 1)])
        grad_middle, rows, grad_gain = norm_backward(
            part(local_cot, micro), middles[micro], terms, gains[1:]
        )
        grad_gain2 = grad_gain2 + grad_gain
        grad_middles.append(grad_middle)
        grad_branches.append(exchange(rows))

    def reduce_rows(grad, blocks):
        blocks = plain(grad.astype(BF16).reshape(blocks, -1, grad.shape[1]))
        return plain(lax.psum_scatter(blocks, "fsdp", scatter_dimension=1, tiled=True))

    def joined(blocks, start, width):
        return blocks[:, :, start : start + width].swapaxes(0, 1).astype(F32).reshape(share, -1)

    def all_micros(parts):
        return jnp.stack(parts, axis=1).reshape(all_rows, parts[0].shape[-1])

    up_product = outer(
        after(all_micros(seconds), grad_seconds[0], *sums), all_micros(grad_boths)
    ).astype(BF16)
    up_grads = reduce_rows(up_product, spans)
    grad_gates, grad_sents, grad_gain, grad_taps, grad_small = [], [], 0.0, 0.0, 0.0
    for micro in range(micros):
        mixed, update, inverse = mixers[micro]
        grad = after(grad_branches[micro], *grad_sents)
        grad = dot_back(grad.reshape(-1, D), w_out).reshape(spans, 1, length, vw)
        grad_mixed, grad_gate, term = gate_backward(micro, mixed, gate, gain_row, grad, heads)
        if micro + 1 == micros:
            grad_mixed = after(grad_mixed, up_grads)
        grad_sent, term_taps, term_small = mixer_backward(
            micro, pack_lengths, rates, sent, taps, update, inverse, grad_mixed, heads
        )
        grad_gates.append(grad_gate.reshape(spans, length, vw))
        grad_sents.append(grad_sent.reshape(spans, length, mix_width))
        grad_gain, grad_taps = grad_gain + term, grad_taps + term_taps
        grad_small = grad_small + term_small
    finals, wait = [], grad_sents[0]
    for micro in range(micros):
        wait = scatter_rows(after(final_rows[micro], wait), spans)
        finals.append(wait)
    block_out = jnp.stack([
        middle + jnp.sum(terms.astype(F32), axis=0) for middle, terms in zip(middles, finals)
    ]).reshape(local_rows, D)

    grad_proj = all_micros([
        jnp.concatenate(pair, axis=-1) for pair in zip(grad_sents, grad_gates)
    ])
    grad_down = lax.psum_scatter(
        after(down_grads, grad_middles[0]), "fsdp", scatter_dimension=0
    )
    in_product = outer(after(first, finals[0]), grad_proj)
    in_grads = reduce_rows(in_product, spans)
    grad_proj = after(grad_proj, in_product)
    grad_first = dot_back(grad_proj[:, :mix_width], w_mix) + dot_back(
        grad_proj[:, mix_width:], w_gate
    )
    grad_gain1 = jnp.sum(inputs * input_scale * grad_first, axis=0)
    first_rows = grad_first.astype(BF16)
    grad_first = scatter_rows(after(first_rows, grad_down, up_grads), spans)
    out_grads = outer(
        all_micros([n[:, 0] for n in normeds]), after(all_micros(grad_branches), first_rows)
    )
    grad_out = lax.psum_scatter(
        out_grads.astype(BF16), "fsdp", scatter_dimension=0, tiled=True
    ).astype(F32)
    gain_rows = jnp.stack([grad_gain1, grad_gain2[0]])
    flat = jnp.concatenate([
        grad_taps[:, :pair_at].reshape(-1), gain_rows.reshape(-1), grad_gain.reshape(-1),
        grad_small[:2].reshape(-1),
    ])
    flat = jnp.pad(flat, (0, round_up(flat.size, 8 * LANES) - flat.size)).reshape(-1, LANES)
    flat = lax.psum(after(flat, grad_gain1), "fsdp")
    flat = lax.all_gather(flat, "seq", axis=0).reshape(spans, -1)
    grad_norm1, _ = norm_back(
        local_tokens.astype(F32), gains[0], jnp.sum(grad_first.astype(F32), axis=0)
    )
    grad_tokens = jnp.stack(grad_middles).reshape(local_rows, D) + grad_norm1
    up_grads, flat = lax.optimization_barrier((up_grads, flat))
    up_grads = exchange(after(up_grads, grad_first))
    in_grads = exchange(after(in_grads, up_grads))
    grad_up = jnp.concatenate([joined(up_grads, 0, fw), joined(up_grads, fp, fw)], axis=1)
    grad_in = jnp.concatenate(
        [
            joined(in_grads, 0, qw),
            joined(in_grads, qw, qw),
            joined(in_grads, 2 * qw, vw),
            joined(in_grads, mix_width, vw),
        ],
        axis=1,
    )
    grad_decay = joined(in_grads, pair_at, 2 * heads)

    taps_flat = flat[:, : CONV * pair_at].reshape(spans, CONV, pair_at)

    def all_taps(start, width):
        return taps_flat[:, :, start : start + width].swapaxes(0, 1).reshape(CONV, -1)

    grad_conv = jnp.concatenate(
        [all_taps(0, qw), all_taps(qw, qw), all_taps(2 * qw, vw)], axis=1
    )
    index = place * packs + lax.axis_index("fsdp")
    grad_conv = cut(grad_conv, index * conv_share, conv_share, 1).T
    at = CONV * pair_at
    gains_flat = jnp.sum(flat[:, at : at + 2 * D], axis=0).reshape(2, D)
    gain_share = norm_gains.shape[1]
    grad_gains = cut(gains_flat, index * gain_share, gain_share, 1)
    at = at + 2 * D
    grad_gain = jnp.sum(flat[:, at : at + DV], axis=0)
    at = at + DV
    return (
        block_out.astype(BF16).reshape(micros, 1, length, D),
        grad_tokens.reshape(micros, 1, length, D),
        grad_in,
        grad_decay,
        grad_conv,
        flat[:, at : at + heads].reshape(H),
        flat[:, at + LANES : at + LANES + heads].reshape(H),
        grad_gains,
        grad_gain,
        grad_out,
        grad_up,
        grad_down.astype(F32),
    )


def solution(mesh):
    rows = P(("seq", "fsdp"), None)
    packs = P(None, "fsdp", "seq", None)
    gains = P(None, ("seq", "fsdp"))
    return jax.shard_map(
        shards,
        mesh=mesh,
        in_specs=(
            packs, P(None, "fsdp", None), rows, rows, rows, P(), P(), gains, P(), rows, rows, rows,
            packs,
        ),
        out_specs=(packs, packs, rows, rows, rows, P(), P(), gains, P(), rows, rows, rows),
        check_vma=False,
    )
```

```python
from functools import partial

import jax
import jax.numpy as jnp
from jax import lax
from jax.experimental import pallas as pl
from jax.experimental.layout import Layout, with_layout_constraint
from jax.experimental.pallas import tpu as pltpu
from jax.sharding import PartitionSpec as P

D = 2048
H = 16
DK = 128
DV = 256
FF = 5504
CONV = 4
EPS = 1e-06
BLOCK = 128
LANES = 128
F32 = jnp.float32
BF16 = jnp.bfloat16


def round_up(value, step):
    return -(-value // step) * step


NN = (((1,), (0,)), ((), ()))
NT = (((1,), (1,)), ((), ()))
TN = (((0,), (0,)), ((), ()))


def dot1(left, right, form=NN):
    return lax.dot_general(
        left.astype(BF16), right.astype(BF16), form, preferred_element_type=F32
    )


def halves(value):
    high = value.astype(BF16)
    return high, (value - high.astype(F32)).astype(BF16)


def dot3(left, right, form=NN):
    left_high, left_low = halves(left)
    right_high, right_low = halves(right)
    dot = partial(lax.dot_general, dimension_numbers=form, preferred_element_type=F32)
    return dot(left_high, right_high) + (dot(left_high, right_low) + dot(left_low, right_high))


def sigmoid(value):
    return 1.0 / (1.0 + jnp.exp(-value))


def pack_masks(ends, count):
    place = lax.broadcasted_iota(jnp.int32, (count, 1), 0)
    start = jnp.zeros((count, 1), jnp.int32)
    for end in ends:
        start = jnp.where(place >= end, jnp.maximum(start, end), start)
    rows = lax.broadcasted_iota(jnp.int32, (count, count), 0)
    cols = lax.broadcasted_iota(jnp.int32, (count, count), 1)
    return place, start, rows, cols


def conv_silu(raw, taps, place, start):
    total = raw * taps[CONV - 1 : CONV]
    for lag in range(1, CONV):
        moved = pltpu.roll(raw, lag, 0)
        same = place - lag >= start
        total = total + jnp.where(same, moved, 0.0) * taps[CONV - 1 - lag : CONV - lag]
    gate = sigmoid(total)
    return total, gate, total * gate


def conv_silu_back(grad, total, gate, raw, taps, place, start):
    grad_total = grad * gate * (1.0 + total * (1.0 - gate))
    grad_raw = grad_total * taps[CONV - 1 : CONV]
    grad_taps = [None] * CONV
    grad_taps[CONV - 1] = jnp.sum(grad_total * raw, axis=0, keepdims=True)
    count = raw.shape[0]
    for lag in range(1, CONV):
        same = place - lag >= start
        kept = jnp.where(same, grad_total, 0.0)
        moved = pltpu.roll(raw, lag, 0)
        grad_taps[CONV - 1 - lag] = jnp.sum(kept * moved, axis=0, keepdims=True)
        grad_raw = grad_raw + pltpu.roll(kept, count - lag, 0) * taps[CONV - 1 - lag : CONV - lag]
    return grad_raw, grad_taps


def unit_rows(values):
    scale = lax.rsqrt(jnp.sum(values * values, axis=1, keepdims=True) + EPS)
    return values * scale, scale


def unit_rows_back(grad, values, scale):
    inner = jnp.sum(values * grad, axis=1, keepdims=True)
    return scale * grad - values * (scale * scale * scale * inner)


def column(values, lanes, index):
    return jnp.sum(jnp.where(lanes == index, values, 0.0), axis=1, keepdims=True)


def decay_grid(log_rate, start, rows, cols):
    count = log_rate.shape[0]
    lower = jnp.where(cols <= rows, 1.0, 0.0).astype(BF16)
    spread = jnp.where(cols < rows, jnp.broadcast_to(log_rate, (count, count)), 0.0)
    first = spread.astype(BF16)
    rest = spread - first.astype(F32)
    second = rest.astype(BF16)
    third = (rest - second.astype(F32)).astype(BF16)
    dot = partial(lax.dot_general, dimension_numbers=NN, preferred_element_type=F32)
    summed = dot(lower, first) + (dot(lower, second) + dot(lower, third))
    inside = (cols <= rows) & (cols >= start)
    return jnp.where(inside, jnp.exp(jnp.where(inside, summed, 0.0)), 0.0)


def unit_lower_inverses(blocks):
    size = blocks[0].shape[0]
    rows = lax.broadcasted_iota(jnp.int32, (size, size), 0)
    cols = lax.broadcasted_iota(jnp.int32, (size, size), 1)
    level, results = 0, []
    while (1 << level) < size:
        width = 1 << level
        joint = (
            ((rows >> (level + 1)) == (cols >> (level + 1)))
            & ((rows & width) != 0)
            & ((cols & width) == 0)
        )
        parts = [jnp.where(joint, block, 0.0) for block in blocks]
        if level == 0:
            unit = jnp.where(rows == cols, 1.0, 0.0).astype(F32)
            results = [unit - part for part in parts]
        else:
            inner = [dot3(part, result) for part, result in zip(parts, results)]
            results = [result - dot3(result, term) for result, term in zip(results, inner)]
        level += 1
    return results


def read_rows(ref, offset, width):
    shape = ref.shape
    return ref[:, 0, :, pl.ds(offset, width)].reshape(shape[0] * shape[2], width)


def write_rows(ref, offset, value):
    shape = ref.shape
    ref[:, 0, :, pl.ds(offset, value.shape[1])] = value.reshape(
        shape[0], shape[2], value.shape[1]
    ).astype(ref.dtype)


def pack_ends(lengths_ref, micro, docs):
    ends, total = [], 0
    for index in range(docs - 1):
        total = total + lengths_ref[micro, index]
        ends.append(total)
    return ends


def head_inputs(sent_ref, taps_ref, rate_ref, head, heads, place, start):
    qw = heads * DK
    out = {}
    for name, offset, width in (
        ("q", head * DK, DK),
        ("k", qw + head * DK, DK),
        ("v", 2 * qw + head * DV, DV),
    ):
        offset = pl.multiple_of(offset, LANES)
        raw = read_rows(sent_ref, offset, width).astype(F32)
        taps = taps_ref[:, pl.ds(offset, width)]
        out[name] = (offset, raw, taps) + conv_silu(raw, taps, place, start)
    offset = 2 * qw + heads * DV
    pairs = read_rows(sent_ref, offset, LANES).astype(F32)
    lanes = lax.broadcasted_iota(jnp.int32, pairs.shape, 1)
    decay_in = column(pairs, lanes, 2 * head) + rate_ref[1, head]
    soft = jnp.maximum(decay_in, 0.0) + jnp.log1p(jnp.exp(-jnp.abs(decay_in)))
    out["log"] = rate_ref[0, head] * soft
    out["decay_in"] = decay_in
    out["beta"] = sigmoid(column(pairs, lanes, 2 * head + 1))
    out["lanes"] = lanes
    return out


def mixer_forward_kernel(
    micro, per_step, heads, docs, lengths_ref, rate_ref, sent_ref, taps_ref,
    mixed_ref, update_ref, inverse_ref,
):
    count = sent_ref.shape[0] * sent_ref.shape[2]
    place, start, rows, cols = pack_masks(pack_ends(lengths_ref, micro, docs), count)
    blocks = count // BLOCK
    parts = []
    for local in range(per_step):
        head = pl.program_id(0) * per_step + local
        made = head_inputs(sent_ref, taps_ref, rate_ref, head, heads, place, start)
        query = unit_rows(made["q"][5])[0] * DK ** (-0.5)
        keys = unit_rows(made["k"][5])[0]
        beta = made["beta"]
        decay = decay_grid(made["log"], start, rows, cols)
        system = jnp.where(cols < rows, decay, 0.0) * beta * dot3(keys, keys, NT)
        parts.append((system, beta * made["v"][5], decay * dot1(query, keys, NT)))
    spans = [slice(block * BLOCK, (block + 1) * BLOCK) for block in range(blocks)]
    inverses = unit_lower_inverses([system[at, at] for system, _, _ in parts for at in spans])
    for local in range(per_step):
        system, target, scores = parts[local]
        updates = []
        for block, at in enumerate(spans):
            inverse = inverses[local * blocks + block]
            inverse_ref[local, block] = inverse
            right = target[at]
            for earlier in range(block):
                right = right - dot3(system[at, spans[earlier]], updates[earlier])
            updates.append(dot3(inverse, right))
        update = jnp.concatenate(updates, axis=0)
        update_ref[local] = update
        head = pl.program_id(0) * per_step + local
        write_rows(mixed_ref, pl.multiple_of(head * DV, LANES), dot1(scores, update))


def mixer_backward_kernel(
    micro, per_step, heads, docs, lengths_ref, rate_ref, sent_ref, taps_ref,
    update_ref, inverse_ref, grad_ref,
    grad_sent_ref, grad_taps_ref, small_ref,
):
    count = sent_ref.shape[0] * sent_ref.shape[2]
    place, start, rows, cols = pack_masks(pack_ends(lengths_ref, micro, docs), count)
    blocks = count // BLOCK
    pair_offset = 2 * heads * DK + heads * DV

    @pl.when(pl.program_id(0) == 0)
    def _():
        small_ref[...] = jnp.zeros_like(small_ref)
        grad_taps_ref[...] = jnp.zeros_like(grad_taps_ref)
        write_rows(grad_sent_ref, pair_offset, jnp.zeros((count, LANES), BF16))

    grad_pairs = read_rows(grad_sent_ref, pair_offset, LANES).astype(F32)
    small_lanes = lax.broadcasted_iota(jnp.int32, (1, LANES), 1)
    for local in range(per_step):
        head = pl.program_id(0) * per_step + local
        made = head_inputs(sent_ref, taps_ref, rate_ref, head, heads, place, start)
        unit_q, scale_q = unit_rows(made["q"][5])
        query = unit_q * DK ** (-0.5)
        keys, scale_k = unit_rows(made["k"][5])
        values = made["v"][5]
        beta = made["beta"]
        grad_mixed = read_rows(grad_ref, pl.multiple_of(head * DV, LANES), DV)
        decay = decay_grid(made["log"], start, rows, cols)
        strict = jnp.where(cols < rows, decay, 0.0)
        keys_keys = dot3(keys, keys, NT)
        weighted = strict * beta
        system = weighted * keys_keys
        scores = decay * dot1(query, keys, NT)
        update = update_ref[local]
        grad_scores = dot1(grad_mixed, update, NT)
        grad_update = dot1(scores, grad_mixed, TN)
        grad_targets = [None] * blocks
        for block in reversed(range(blocks)):
            at = slice(block * BLOCK, (block + 1) * BLOCK)
            right = grad_update[at]
            for later in range(block + 1, blocks):
                right = right - dot3(
                    system[later * BLOCK : (later + 1) * BLOCK, at], grad_targets[later], TN
                )
            grad_targets[block] = dot3(inverse_ref[local, block], right, TN)
        grad_target = jnp.concatenate(grad_targets, axis=0)
        grad_system = -dot1(grad_target, update, NT)
        grad_values = beta * grad_target
        grad_beta = jnp.sum(grad_target * values, axis=1, keepdims=True) + jnp.sum(
            grad_system * strict * keys_keys, axis=1, keepdims=True
        )
        grad_kk = grad_system * weighted
        grad_qk = grad_scores * decay
        grad_query = dot1(grad_qk, keys) * DK ** (-0.5)
        grad_keys = dot1(grad_kk, keys) + dot1(grad_kk, keys, TN) + dot1(grad_qk, query, TN)
        grad_spread = grad_scores * scores + grad_system * system
        lower = jnp.where(cols <= rows, 1.0, 0.0).astype(BF16)
        high, low = halves(grad_spread)
        dot = partial(lax.dot_general, dimension_numbers=TN, preferred_element_type=F32)
        after = dot(lower, high) + dot(lower, low)
        grad_log = jnp.sum(jnp.where(cols < rows, after, 0.0), axis=1, keepdims=True)
        grad_decay = grad_log * rate_ref[0, head] * sigmoid(made["decay_in"])
        grad_beta_in = grad_beta * beta * (1.0 - beta)
        lanes = made["lanes"]
        grad_pairs = jnp.where(lanes == 2 * head, grad_decay, grad_pairs)
        grad_pairs = jnp.where(lanes == 2 * head + 1, grad_beta_in, grad_pairs)
        grad_alog = jnp.sum(grad_log * made["log"], axis=0, keepdims=True)
        grad_dt = jnp.sum(grad_decay, axis=0, keepdims=True)
        small_ref[0:1] += jnp.where(small_lanes == head, grad_alog, 0.0)
        small_ref[1:2] += jnp.where(small_lanes == head, grad_dt, 0.0)
        for name, grad in (
            ("q", unit_rows_back(grad_query, made["q"][5], scale_q)),
            ("k", unit_rows_back(grad_keys, made["k"][5], scale_k)),
            ("v", grad_values),
        ):
            where, raw, taps, total, opened, _ = made[name]
            grad_raw, grad_taps = conv_silu_back(grad, total, opened, raw, taps, place, start)
            write_rows(grad_sent_ref, where, grad_raw)
            for tap in range(CONV):
                grad_taps_ref[tap : tap + 1, pl.ds(where, raw.shape[1])] += grad_taps[tap]
    write_rows(grad_sent_ref, pair_offset, grad_pairs)


def gate_forward_kernel(heads, mixed_ref, gate_ref, gain_ref, normed_ref):
    for head in range(heads):
        offset = head * DV
        mixed = read_rows(mixed_ref, offset, DV).astype(F32)
        gate = read_rows(gate_ref, offset, DV)
        scale = lax.rsqrt(jnp.mean(mixed * mixed, axis=1, keepdims=True) + EPS)
        write_rows(normed_ref, offset, mixed * scale * gain_ref[...] * (gate * sigmoid(gate)))


def gate_backward_kernel(
    heads, mixed_ref, gate_ref, gain_ref, grad_ref, grad_mixed_ref, grad_gate_ref, grad_gain_ref
):
    @pl.when(pl.program_id(0) == 0)
    def _():
        grad_gain_ref[...] = jnp.zeros_like(grad_gain_ref)

    gain = gain_ref[...]
    for head in range(heads):
        offset = head * DV
        mixed = read_rows(mixed_ref, offset, DV).astype(F32)
        gate = read_rows(gate_ref, offset, DV)
        grad = read_rows(grad_ref, offset, DV)
        scale = lax.rsqrt(jnp.mean(mixed * mixed, axis=1, keepdims=True) + EPS)
        soft = sigmoid(gate)
        plain_rows = mixed * scale
        write_rows(
            grad_gate_ref, offset, grad * plain_rows * gain * soft * (1.0 + gate * (1.0 - soft))
        )
        grad = grad * (gate * soft)
        grad_gain_ref[...] += jnp.sum(grad * plain_rows, axis=0, keepdims=True)
        grad = grad * gain
        inner = jnp.mean(mixed * grad, axis=1, keepdims=True)
        write_rows(
            grad_mixed_ref, offset, scale * grad - mixed * (scale * scale * scale * inner)
        )


def pack_kernel(query_ref, key_ref, value_ref, pairs_ref, gate_ref, out_ref):
    at = 0
    for ref in (query_ref, key_ref, value_ref, pairs_ref, gate_ref):
        block = ref[...].reshape(out_ref.shape[1], ref.shape[-1])
        out_ref[0, :, at : at + ref.shape[-1]] = block
        at += ref.shape[-1]


def pack_columns(weight, pairs, spans):
    rows = weight.shape[0]
    qw, vw = H * DK // spans, H * DV // spans
    width = 2 * qw + 2 * vw + pairs.shape[2]
    start = 2 * H * DK // vw

    def spec(columns, first):
        return pl.BlockSpec((rows, columns), lambda s: (0, first + s))

    return pl.pallas_call(
        pack_kernel,
        grid=(spans,),
        in_specs=[
            spec(qw, 0), spec(qw, spans), spec(vw, start),
            pl.BlockSpec((1, rows, pairs.shape[2]), lambda s: (s, 0, 0)),
            spec(vw, start + spans),
        ],
        out_specs=pl.BlockSpec((1, rows, width), lambda s: (s, 0, 0)),
        out_shape=jax.ShapeDtypeStruct((spans, rows, width), BF16),
        name="pack_columns",
    )(weight, weight, weight, pairs, weight)


def row_spec(array, micro):
    spans, micros, length, width = array.shape
    pick = micro if micros > 1 else 0
    return pl.BlockSpec((spans, 1, length, width), lambda h: (0, pick, 0, 0))


def span_spec(array, micro):
    _, micros, length, width = array.shape
    pick = micro if micros > 1 else 0
    return pl.BlockSpec((1, 1, length, width), lambda s: (s, pick, 0, 0))


def whole_spec(*dims):
    return pl.BlockSpec(dims, lambda h: (0,) * len(dims))


def mixer_cost(sent, heads, passes):
    count = sent.shape[0] * sent.shape[2]
    return pl.CostEstimate(
        flops=passes * heads * 2 * count * count * DV,
        bytes_accessed=passes * heads * count * count * 4,
        transcendentals=heads * count * count,
    )


def mixer_forward(micro, lengths, rates, sent, taps, heads):
    spans, _, length, width = sent.shape
    count, per_step = spans * length, 4 if heads % 4 == 0 else 1 + (heads % 2 == 0)
    blocks = count // BLOCK
    smem = pl.BlockSpec(memory_space=pltpu.SMEM)
    mixed = jax.ShapeDtypeStruct((spans, 1, length, heads * DV), BF16)
    return pl.pallas_call(
        partial(mixer_forward_kernel, micro, per_step, heads, lengths.shape[1]),
        grid=(heads // per_step,),
        in_specs=[smem, smem, row_spec(sent, micro), whole_spec(CONV, width)],
        out_specs=[
            row_spec(mixed, 0),
            pl.BlockSpec((per_step, count, DV), lambda h: (h, 0, 0)),
            pl.BlockSpec((per_step, blocks, BLOCK, BLOCK), lambda h: (h, 0, 0, 0)),
        ],
        out_shape=[
            mixed,
            jax.ShapeDtypeStruct((heads, count, DV), F32),
            jax.ShapeDtypeStruct((heads, blocks, BLOCK, BLOCK), F32),
        ],
        compiler_params=pltpu.CompilerParams(vmem_limit_bytes=40 * 1024 * 1024),
        cost_estimate=mixer_cost(sent, heads, 300),
        name="mixer_forward",
    )(lengths, rates, sent, taps)


def mixer_backward(micro, lengths, rates, sent, taps, update, inverse, grad, heads):
    spans, _, length, width = sent.shape
    count, per_step = spans * length, 2 if heads % 2 == 0 else 1
    blocks = count // BLOCK
    smem = pl.BlockSpec(memory_space=pltpu.SMEM)
    grad_sent = jax.ShapeDtypeStruct((spans, 1, length, width), BF16)
    return pl.pallas_call(
        partial(mixer_backward_kernel, micro, per_step, heads, lengths.shape[1]),
        grid=(heads // per_step,),
        in_specs=[
            smem, smem, row_spec(sent, micro), whole_spec(CONV, width),
            pl.BlockSpec((per_step, count, DV), lambda h: (h, 0, 0)),
            pl.BlockSpec((per_step, blocks, BLOCK, BLOCK), lambda h: (h, 0, 0, 0)),
            row_spec(grad, 0),
        ],
        out_specs=[row_spec(grad_sent, 0), whole_spec(CONV, width), whole_spec(8, LANES)],
        out_shape=[
            grad_sent,
            jax.ShapeDtypeStruct((CONV, width), F32),
            jax.ShapeDtypeStruct((8, LANES), F32),
        ],
        compiler_params=pltpu.CompilerParams(vmem_limit_bytes=40 * 1024 * 1024),
        cost_estimate=mixer_cost(sent, heads, 40),
        name="mixer_backward",
    )(lengths, rates, sent, taps, update, inverse, grad)


def gate_forward(micro, mixed, gate, gain, heads):
    return pl.pallas_call(
        partial(gate_forward_kernel, heads),
        grid=(mixed.shape[0],),
        in_specs=[span_spec(mixed, 0), span_spec(gate, micro), whole_spec(1, DV)],
        out_specs=span_spec(mixed, 0),
        out_shape=jax.ShapeDtypeStruct(mixed.shape, BF16),
        cost_estimate=pl.CostEstimate(
            flops=20 * mixed.size, bytes_accessed=8 * mixed.size, transcendentals=mixed.size
        ),
        name="gate_forward",
    )(mixed, gate, gain)


def gate_backward(micro, mixed, gate, gain, grad, heads):
    out = jax.ShapeDtypeStruct(mixed.shape, BF16)
    return pl.pallas_call(
        partial(gate_backward_kernel, heads),
        grid=(mixed.shape[0],),
        in_specs=[
            span_spec(mixed, 0), span_spec(gate, micro), whole_spec(1, DV), span_spec(grad, 0),
        ],
        out_specs=[span_spec(out, 0), span_spec(out, 0), whole_spec(1, DV)],
        out_shape=[out, out, jax.ShapeDtypeStruct((1, DV), F32)],
        cost_estimate=pl.CostEstimate(
            flops=40 * mixed.size, bytes_accessed=100 * mixed.size, transcendentals=mixed.size
        ),
        name="gate_backward",
    )(mixed, gate, gain, grad)


def norm_forward_kernel(base_ref, terms_ref, gain_ref, middle_ref, rows_ref):
    middle = base_ref[...].astype(F32)
    for span in range(terms_ref.shape[0]):
        middle = middle + terms_ref[span].astype(F32)
    scale = lax.rsqrt(jnp.mean(middle * middle, axis=1, keepdims=True) + EPS)
    rows = (middle * scale * gain_ref[...]).astype(BF16)
    middle_ref[...] = middle
    for span in range(rows_ref.shape[0]):
        rows_ref[span] = rows


def norm_backward_kernel(
    base_ref, middle_ref, terms_ref, gain_ref, grad_ref, rows_ref, grad_gain_ref
):
    middle = middle_ref[...]
    grad = terms_ref[0].astype(F32)
    for span in range(1, terms_ref.shape[0]):
        grad = grad + terms_ref[span].astype(F32)
    scale = lax.rsqrt(jnp.mean(middle * middle, axis=1, keepdims=True) + EPS)
    grad_gain_ref[...] = jnp.sum(middle * scale * grad, axis=0, keepdims=True)
    inner = grad * gain_ref[...]
    weight = scale * scale * scale * jnp.mean(middle * inner, axis=1, keepdims=True)
    total = base_ref[...].astype(F32) + scale * inner - middle * weight
    grad_ref[...] = total
    rows = total.astype(BF16)
    for span in range(rows_ref.shape[0]):
        rows_ref[span] = rows


def norm_forward(base, terms, gain):
    return pl.pallas_call(
        norm_forward_kernel,
        out_shape=[
            jax.ShapeDtypeStruct(base.shape, F32),
            jax.ShapeDtypeStruct(terms.shape, BF16),
        ],
        cost_estimate=pl.CostEstimate(
            flops=20 * base.size, bytes_accessed=40 * base.size, transcendentals=0
        ),
        name="norm_forward",
    )(base, terms, gain)


def norm_backward(base, middle, terms, gain):
    return pl.pallas_call(
        norm_backward_kernel,
        out_shape=[
            jax.ShapeDtypeStruct(base.shape, F32),
            jax.ShapeDtypeStruct(terms.shape, BF16),
            jax.ShapeDtypeStruct(gain.shape, F32),
        ],
        cost_estimate=pl.CostEstimate(
            flops=30 * base.size, bytes_accessed=40 * base.size, transcendentals=0
        ),
        name="norm_backward",
    )(base, middle, terms, gain)


def dot(left, right):
    return jnp.dot(left, right, preferred_element_type=F32)


def outer(left, right):
    return lax.dot_general(left, right, TN, preferred_element_type=F32)


def dot_back(left, right):
    return lax.dot_general(left, right, NT, preferred_element_type=F32)


def after(value, *earlier):
    return lax.optimization_barrier((value,) + earlier)[0]


def plain(array):
    return with_layout_constraint(array, Layout(major_to_minor=tuple(range(array.ndim))))


def exchange(blocks):
    return lax.all_to_all(blocks, "seq", split_axis=0, concat_axis=0, tiled=True)


def gather_rows(rows, *earlier):
    spans = lax.axis_size("seq")
    copies = jnp.broadcast_to(rows[None], (spans,) + rows.shape)
    return exchange(after(lax.optimization_barrier(copies), *earlier))


def scatter_rows(partial_rows, spans):
    return exchange(
        partial_rows.astype(BF16).reshape((spans, -1) + partial_rows.shape[1:])
    )


def cut(array, start, size, axis=0):
    return lax.dynamic_slice_in_dim(array, start, size, axis, allow_negative_indices=False)


def norm_scale(values):
    return lax.rsqrt(jnp.mean(values * values, axis=-1, keepdims=True) + EPS)


def norm_back(values, gain, grad):
    scale = norm_scale(values)
    inner = gain * grad
    back = scale * inner - values * (
        scale * scale * scale * jnp.mean(values * inner, axis=-1, keepdims=True)
    )
    return back, jnp.sum(values * scale * grad, axis=0)


def shards(
    tokens, lengths, in_weight, decay_weight, conv_weight, a_log, dt_bias, norm_gains, out_gain,
    out_weight, up_weight, down_weight, cotangent,
):
    spans, packs = lax.axis_size("seq"), lax.axis_size("fsdp")
    place = lax.axis_index("seq")
    micros, _, length, _ = tokens.shape
    heads = H // spans
    qw, vw, fw = heads * DK, heads * DV, FF // spans
    fp = round_up(fw, LANES)
    share = in_weight.shape[0]
    local_rows = micros * length

    def columns(array, start, count):
        return array[:, start : start + count * spans].reshape(share, spans, count)

    def widen(array, count):
        return jnp.pad(array, ((0, 0), (0, 0), (0, count - array.shape[2])))

    def by_span(pieces):
        return jnp.concatenate(pieces, axis=2).swapaxes(0, 1)

    def gather_weight(blocks):
        full = plain(lax.all_gather(plain(blocks), "fsdp", axis=1, tiled=True))
        return full.reshape(D, blocks.shape[2])

    conv_share = conv_weight.shape[0]
    conv_cols = CONV * conv_share // share
    small = jnp.concatenate([conv_weight.reshape(share, conv_cols), norm_gains.T], axis=1)
    small = jnp.broadcast_to(small[:, None], (share, spans, conv_cols + 2))
    pairs = jnp.concatenate([decay_weight.reshape(share, spans, 2 * heads), small], axis=2)
    pair_at = 2 * qw + vw
    mix_width = pair_at + LANES
    in_blocks = pack_columns(in_weight, widen(pairs, LANES).swapaxes(0, 1), spans)
    up_blocks = by_span([
        widen(columns(up_weight, 0, fw), fp),
        widen(columns(up_weight, FF, fw), fp),
    ])
    local_tokens = tokens.reshape(local_rows, D)
    local_cot = cotangent.reshape(local_rows, D)
    grouped = (spans, micros, length)
    all_rows = spans * local_rows

    in_blocks, up_blocks = lax.optimization_barrier((exchange(in_blocks), up_blocks))
    w_mix = gather_weight(in_blocks[:, :, :mix_width])
    all_tokens = gather_rows(local_tokens, in_blocks)

    cot = gather_rows(local_cot, all_tokens).reshape(all_rows, D)
    small_at = pair_at + 2 * heads
    small = plain(w_mix[:, small_at : small_at + conv_cols + 2])
    gains = small[:, conv_cols:].T.astype(F32)

    def own(base, width):
        step = conv_share // share
        rows = cut(small[:, :conv_cols], base // step + place * (width // step), width // step)
        return rows.reshape(width, CONV).T

    taps = jnp.concatenate(
        [own(0, qw), own(H * DK, qw), own(2 * H * DK, vw), jnp.zeros((CONV, LANES), BF16)],
        axis=1,
    ).astype(F32)
    rates = jnp.stack([
        -jnp.exp(cut(a_log, place * heads, heads)),
        cut(dt_bias, place * heads, heads),
    ])
    gain_row = out_gain.reshape(1, DV)
    pack_lengths = lengths[:, 0]

    inputs = all_tokens.reshape(all_rows, D).astype(F32)
    input_scale = norm_scale(inputs)
    first = (inputs * input_scale * gains[0]).astype(BF16)
    sent = dot(first, w_mix).astype(BF16)
    w_gate = gather_weight(after(in_blocks[:, :, mix_width:], all_tokens))
    w_down = lax.all_gather(after(down_weight, w_mix), "fsdp", axis=0)
    w_out = lax.all_gather(after(out_weight, w_mix), "fsdp", axis=0, tiled=True)
    sent = sent.reshape(grouped + (mix_width,))
    mixers = []
    for micro in range(micros):
        mixers.append(
            mixer_forward(micro, pack_lengths, rates, sent, taps, heads)
        )
        sent = after(sent, mixers[-1][0])
    up_blocks = exchange(after(up_blocks, cot, mixers[0][0]))
    w_down = lax.optimization_barrier(w_down.reshape(fw, D))
    gate = dot(first, w_gate).reshape(grouped + (vw,))
    grad_act = dot_back(cot, w_down).reshape(grouped + (fw,))

    def part(array, micro):
        return array.reshape((micros, length) + array.shape[1:])[micro]

    normeds, branches, branch_rows = [], [], []
    for micro in range(micros):
        normeds.append(gate_forward(micro, mixers[micro][0], gate, gain_row, heads))
        rows = dot(normeds[-1].reshape(-1, vw), w_out).astype(BF16)
        branches.append(scatter_rows(after(rows, up_blocks), spans))
        branch_rows.append(rows)
    w_up = gather_weight(after(up_blocks, branch_rows[0]))
    middles, seconds = [], []
    for micro in range(micros):
        middle, rows = norm_forward(part(local_tokens, micro), branches[micro], gains[1:])
        middles.append(middle)
        seconds.append(exchange(rows))

    acts, grad_boths, grad_seconds, sums = [], [], [], []
    for micro in range(micros):
        seconds[micro] = after(seconds[micro], *sums)
        both = dot(seconds[micro].reshape(-1, D), w_up)
        gated, upper = both[:, :fp], both[:, fp:]
        soft = jax.nn.sigmoid(gated)
        acts.append((gated * soft * upper).astype(BF16).reshape(spans, length, fp))
        grad = jnp.pad(grad_act[:, micro].reshape(-1, fw), ((0, 0), (0, fp - fw)))
        grad_both = jnp.concatenate(
            [
                (grad * upper * soft * (1.0 + gated * (1.0 - soft))).astype(BF16),
                (grad * gated * soft).astype(BF16),
            ],
            axis=1,
        )
        grad_boths.append(grad_both.reshape(spans, length, 2 * fp))
        rows = dot_back(grad_both, w_up).astype(BF16)
        grad_seconds.append(scatter_rows(rows, spans))
        sums.append(rows)
    act = jnp.stack(acts, axis=1).reshape(all_rows, fp)[:, :fw]
    final_rows = [dot(a.reshape(-1, fp)[:, :fw], w_down).astype(BF16) for a in acts]
    down_grads = outer(after(act, act), cot).astype(BF16).reshape(packs, -1, D)
    spare = [final_rows[:1], final_rows[1:] + [down_grads]]
    grad_middles, grad_branches, grad_gain2 = [], [], 0.0
    for micro in range(micros):
        terms = after(grad_seconds[micro], *spare[min(micro, 1)])
        grad_middle, rows, grad_gain = norm_backward(
            part(local_cot, micro), middles[micro], terms, gains[1:]
        )
        grad_gain2 = grad_gain2 + grad_gain
        grad_middles.append(grad_middle)
        grad_branches.append(exchange(rows))

    def reduce_rows(grad, blocks):
        blocks = plain(grad.astype(BF16).reshape(blocks, -1, grad.shape[1]))
        return plain(lax.psum_scatter(blocks, "fsdp", scatter_dimension=1, tiled=True))

    def joined(blocks, start, width):
        return blocks[:, :, start : start + width].swapaxes(0, 1).astype(F32).reshape(share, -1)

    def all_micros(parts):
        return jnp.stack(parts, axis=1).reshape(all_rows, parts[0].shape[-1])

    up_product = outer(
        after(all_micros(seconds), grad_seconds[0], *sums), all_micros(grad_boths)
    ).astype(BF16)
    up_grads = reduce_rows(up_product, spans)
    grad_gates, grad_sents, grad_gain, grad_taps, grad_small = [], [], 0.0, 0.0, 0.0
    for micro in range(micros):
        mixed, update, inverse = mixers[micro]
        grad = after(grad_branches[micro], *grad_sents)
        grad = dot_back(grad.reshape(-1, D), w_out).reshape(spans, 1, length, vw)
        grad_mixed, grad_gate, term = gate_backward(micro, mixed, gate, gain_row, grad, heads)
        if micro + 1 == micros:
            grad_mixed = after(grad_mixed, up_grads)
        grad_sent, term_taps, term_small = mixer_backward(
            micro, pack_lengths, rates, sent, taps, update, inverse, grad_mixed, heads
        )
        grad_gates.append(grad_gate.reshape(spans, length, vw))
        grad_sents.append(grad_sent.reshape(spans, length, mix_width))
        grad_gain, grad_taps = grad_gain + term, grad_taps + term_taps
        grad_small = grad_small + term_small
    finals, wait = [], grad_sents[0]
    for micro in range(micros):
        wait = scatter_rows(after(final_rows[micro], wait), spans)
        finals.append(wait)
    block_out = jnp.stack([
        middle + jnp.sum(terms.astype(F32), axis=0) for middle, terms in zip(middles, finals)
    ]).reshape(local_rows, D)

    grad_proj = all_micros([
        jnp.concatenate(pair, axis=-1) for pair in zip(grad_sents, grad_gates)
    ])
    grad_down = lax.psum_scatter(
        after(down_grads, grad_middles[0]), "fsdp", scatter_dimension=0
    )
    in_product = outer(after(first, finals[0], up_grads), grad_proj)
    in_grads = reduce_rows(in_product, spans)
    grad_proj = after(grad_proj, in_product)
    grad_first = dot_back(grad_proj[:, :mix_width], w_mix) + dot_back(
        grad_proj[:, mix_width:], w_gate
    )
    grad_gain1 = jnp.sum(inputs * input_scale * grad_first, axis=0)
    first_rows = grad_first.astype(BF16)
    grad_first = scatter_rows(after(first_rows, grad_down, up_grads), spans)
    out_grads = outer(
        all_micros([n[:, 0] for n in normeds]), after(all_micros(grad_branches), first_rows)
    )
    grad_out = lax.psum_scatter(
        out_grads.astype(BF16), "fsdp", scatter_dimension=0, tiled=True
    ).astype(F32)
    gain_rows = jnp.stack([grad_gain1, grad_gain2[0]])
    flat = jnp.concatenate([
        grad_taps[:, :pair_at].reshape(-1), gain_rows.reshape(-1), grad_gain.reshape(-1),
        grad_small[:2].reshape(-1),
    ])
    flat = jnp.pad(flat, (0, round_up(flat.size, 8 * LANES) - flat.size)).reshape(-1, LANES)
    flat = lax.psum(after(flat, grad_gain1), "fsdp")
    flat = lax.all_gather(flat, "seq", axis=0).reshape(spans, -1)
    grad_norm1, _ = norm_back(
        local_tokens.astype(F32), gains[0], jnp.sum(grad_first.astype(F32), axis=0)
    )
    grad_tokens = jnp.stack(grad_middles).reshape(local_rows, D) + grad_norm1
    up_grads, flat = lax.optimization_barrier((up_grads, flat))
    up_grads = exchange(after(up_grads, grad_first))
    in_grads = exchange(after(in_grads, up_grads))
    grad_up = jnp.concatenate([joined(up_grads, 0, fw), joined(up_grads, fp, fw)], axis=1)
    grad_in = jnp.concatenate(
        [
            joined(in_grads, 0, qw),
            joined(in_grads, qw, qw),
            joined(in_grads, 2 * qw, vw),
            joined(in_grads, mix_width, vw),
        ],
        axis=1,
    )
    grad_decay = joined(in_grads, pair_at, 2 * heads)

    taps_flat = flat[:, : CONV * pair_at].reshape(spans, CONV, pair_at)

    def all_taps(start, width):
        return taps_flat[:, :, start : start + width].swapaxes(0, 1).reshape(CONV, -1)

    grad_conv = jnp.concatenate(
        [all_taps(0, qw), all_taps(qw, qw), all_taps(2 * qw, vw)], axis=1
    )
    index = place * packs + lax.axis_index("fsdp")
    grad_conv = cut(grad_conv, index * conv_share, conv_share, 1).T
    at = CONV * pair_at
    gains_flat = jnp.sum(flat[:, at : at + 2 * D], axis=0).reshape(2, D)
    gain_share = norm_gains.shape[1]
    grad_gains = cut(gains_flat, index * gain_share, gain_share, 1)
    at = at + 2 * D
    grad_gain = jnp.sum(flat[:, at : at + DV], axis=0)
    at = at + DV
    return (
        block_out.astype(BF16).reshape(micros, 1, length, D),
        grad_tokens.reshape(micros, 1, length, D),
        grad_in,
        grad_decay,
        grad_conv,
        flat[:, at : at + heads].reshape(H),
        flat[:, at + LANES : at + LANES + heads].reshape(H),
        grad_gains,
        grad_gain,
        grad_out,
        grad_up,
        grad_down.astype(F32),
    )


def solution(mesh):
    rows = P(("seq", "fsdp"), None)
    packs = P(None, "fsdp", "seq", None)
    gains = P(None, ("seq", "fsdp"))
    return jax.shard_map(
        shards,
        mesh=mesh,
        in_specs=(
            packs, P(None, "fsdp", None), rows, rows, rows, P(), P(), gains, P(), rows, rows, rows,
            packs,
        ),
        out_specs=(packs, packs, rows, rows, rows, P(), P(), gains, P(), rows, rows, rows),
        check_vma=False,
    )
```

```python
from functools import partial

import jax
import jax.numpy as jnp
from jax import lax
from jax.experimental import pallas as pl
from jax.experimental.layout import Layout, with_layout_constraint
from jax.experimental.pallas import tpu as pltpu
from jax.sharding import PartitionSpec as P

D = 2048
H = 16
DK = 128
DV = 256
FF = 5504
CONV = 4
EPS = 1e-06
BLOCK = 128
LANES = 128
F32 = jnp.float32
BF16 = jnp.bfloat16


def round_up(value, step):
    return -(-value // step) * step


NN = (((1,), (0,)), ((), ()))
NT = (((1,), (1,)), ((), ()))
TN = (((0,), (0,)), ((), ()))


def dot1(left, right, form=NN):
    return lax.dot_general(
        left.astype(BF16), right.astype(BF16), form, preferred_element_type=F32
    )


def halves(value):
    high = value.astype(BF16)
    return high, (value - high.astype(F32)).astype(BF16)


def dot3(left, right, form=NN):
    left_high, left_low = halves(left)
    right_high, right_low = halves(right)
    dot = partial(lax.dot_general, dimension_numbers=form, preferred_element_type=F32)
    return dot(left_high, right_high) + (dot(left_high, right_low) + dot(left_low, right_high))


def sigmoid(value):
    return 1.0 / (1.0 + jnp.exp(-value))


def pack_masks(ends, count):
    place = lax.broadcasted_iota(jnp.int32, (count, 1), 0)
    start = jnp.zeros((count, 1), jnp.int32)
    for end in ends:
        start = jnp.where(place >= end, jnp.maximum(start, end), start)
    rows = lax.broadcasted_iota(jnp.int32, (count, count), 0)
    cols = lax.broadcasted_iota(jnp.int32, (count, count), 1)
    return place, start, rows, cols


def conv_silu(raw, taps, place, start):
    total = raw * taps[CONV - 1 : CONV]
    for lag in range(1, CONV):
        moved = pltpu.roll(raw, lag, 0)
        same = place - lag >= start
        total = total + jnp.where(same, moved, 0.0) * taps[CONV - 1 - lag : CONV - lag]
    gate = sigmoid(total)
    return total, gate, total * gate


def conv_silu_back(grad, total, gate, raw, taps, place, start):
    grad_total = grad * gate * (1.0 + total * (1.0 - gate))
    grad_raw = grad_total * taps[CONV - 1 : CONV]
    grad_taps = [None] * CONV
    grad_taps[CONV - 1] = jnp.sum(grad_total * raw, axis=0, keepdims=True)
    count = raw.shape[0]
    for lag in range(1, CONV):
        same = place - lag >= start
        kept = jnp.where(same, grad_total, 0.0)
        moved = pltpu.roll(raw, lag, 0)
        grad_taps[CONV - 1 - lag] = jnp.sum(kept * moved, axis=0, keepdims=True)
        grad_raw = grad_raw + pltpu.roll(kept, count - lag, 0) * taps[CONV - 1 - lag : CONV - lag]
    return grad_raw, grad_taps


def unit_rows(values):
    scale = lax.rsqrt(jnp.sum(values * values, axis=1, keepdims=True) + EPS)
    return values * scale, scale


def unit_rows_back(grad, values, scale):
    inner = jnp.sum(values * grad, axis=1, keepdims=True)
    return scale * grad - values * (scale * scale * scale * inner)


def column(values, lanes, index):
    return jnp.sum(jnp.where(lanes == index, values, 0.0), axis=1, keepdims=True)


def decay_grid(log_rate, start, rows, cols):
    count = log_rate.shape[0]
    lower = jnp.where(cols <= rows, 1.0, 0.0).astype(BF16)
    spread = jnp.where(cols < rows, jnp.broadcast_to(log_rate, (count, count)), 0.0)
    first = spread.astype(BF16)
    rest = spread - first.astype(F32)
    second = rest.astype(BF16)
    third = (rest - second.astype(F32)).astype(BF16)
    dot = partial(lax.dot_general, dimension_numbers=NN, preferred_element_type=F32)
    summed = dot(lower, first) + (dot(lower, second) + dot(lower, third))
    inside = (cols <= rows) & (cols >= start)
    return jnp.where(inside, jnp.exp(jnp.where(inside, summed, 0.0)), 0.0)


def unit_lower_inverses(blocks):
    size = blocks[0].shape[0]
    rows = lax.broadcasted_iota(jnp.int32, (size, size), 0)
    cols = lax.broadcasted_iota(jnp.int32, (size, size), 1)
    level, results = 0, []
    while (1 << level) < size:
        width = 1 << level
        joint = (
            ((rows >> (level + 1)) == (cols >> (level + 1)))
            & ((rows & width) != 0)
            & ((cols & width) == 0)
        )
        parts = [jnp.where(joint, block, 0.0) for block in blocks]
        if level == 0:
            unit = jnp.where(rows == cols, 1.0, 0.0).astype(F32)
            results = [unit - part for part in parts]
        else:
            inner = [dot3(part, result) for part, result in zip(parts, results)]
            results = [result - dot3(result, term) for result, term in zip(results, inner)]
        level += 1
    return results


def read_rows(ref, offset, width):
    shape = ref.shape
    return ref[:, 0, :, pl.ds(offset, width)].reshape(shape[0] * shape[2], width)


def write_rows(ref, offset, value):
    shape = ref.shape
    ref[:, 0, :, pl.ds(offset, value.shape[1])] = value.reshape(
        shape[0], shape[2], value.shape[1]
    ).astype(ref.dtype)


def pack_ends(lengths_ref, micro, docs):
    ends, total = [], 0
    for index in range(docs - 1):
        total = total + lengths_ref[micro, index]
        ends.append(total)
    return ends


def head_inputs(sent_ref, taps_ref, rate_ref, head, heads, place, start):
    qw = heads * DK
    out = {}
    for name, offset, width in (
        ("q", head * DK, DK),
        ("k", qw + head * DK, DK),
        ("v", 2 * qw + head * DV, DV),
    ):
        offset = pl.multiple_of(offset, LANES)
        raw = read_rows(sent_ref, offset, width).astype(F32)
        taps = taps_ref[:, pl.ds(offset, width)]
        out[name] = (offset, raw, taps) + conv_silu(raw, taps, place, start)
    offset = 2 * qw + heads * DV
    pairs = read_rows(sent_ref, offset, LANES).astype(F32)
    lanes = lax.broadcasted_iota(jnp.int32, pairs.shape, 1)
    decay_in = column(pairs, lanes, 2 * head) + rate_ref[1, head]
    soft = jnp.maximum(decay_in, 0.0) + jnp.log1p(jnp.exp(-jnp.abs(decay_in)))
    out["log"] = rate_ref[0, head] * soft
    out["decay_in"] = decay_in
    out["beta"] = sigmoid(column(pairs, lanes, 2 * head + 1))
    out["lanes"] = lanes
    return out


def mixer_forward_kernel(
    micro, per_step, heads, docs, lengths_ref, rate_ref, sent_ref, taps_ref,
    mixed_ref, update_ref, inverse_ref,
):
    count = sent_ref.shape[0] * sent_ref.shape[2]
    place, start, rows, cols = pack_masks(pack_ends(lengths_ref, micro, docs), count)
    blocks = count // BLOCK
    parts = []
    for local in range(per_step):
        head = pl.program_id(0) * per_step + local
        made = head_inputs(sent_ref, taps_ref, rate_ref, head, heads, place, start)
        query = unit_rows(made["q"][5])[0] * DK ** (-0.5)
        keys = unit_rows(made["k"][5])[0]
        beta = made["beta"]
        decay = decay_grid(made["log"], start, rows, cols)
        system = jnp.where(cols < rows, decay, 0.0) * beta * dot3(keys, keys, NT)
        parts.append((system, beta * made["v"][5], decay * dot1(query, keys, NT)))
    spans = [slice(block * BLOCK, (block + 1) * BLOCK) for block in range(blocks)]
    inverses = unit_lower_inverses([system[at, at] for system, _, _ in parts for at in spans])
    for local in range(per_step):
        system, target, scores = parts[local]
        updates = []
        for block, at in enumerate(spans):
            inverse = inverses[local * blocks + block]
            inverse_ref[local, block] = inverse
            right = target[at]
            for earlier in range(block):
                right = right - dot3(system[at, spans[earlier]], updates[earlier])
            updates.append(dot3(inverse, right))
        update = jnp.concatenate(updates, axis=0)
        update_ref[local] = update
        head = pl.program_id(0) * per_step + local
        write_rows(mixed_ref, pl.multiple_of(head * DV, LANES), dot1(scores, update))


def mixer_backward_kernel(
    micro, per_step, heads, docs, lengths_ref, rate_ref, sent_ref, taps_ref,
    update_ref, inverse_ref, grad_ref,
    grad_sent_ref, grad_taps_ref, small_ref,
):
    count = sent_ref.shape[0] * sent_ref.shape[2]
    place, start, rows, cols = pack_masks(pack_ends(lengths_ref, micro, docs), count)
    blocks = count // BLOCK
    pair_offset = 2 * heads * DK + heads * DV

    @pl.when(pl.program_id(0) == 0)
    def _():
        small_ref[...] = jnp.zeros_like(small_ref)
        grad_taps_ref[...] = jnp.zeros_like(grad_taps_ref)
        write_rows(grad_sent_ref, pair_offset, jnp.zeros((count, LANES), BF16))

    grad_pairs = read_rows(grad_sent_ref, pair_offset, LANES).astype(F32)
    small_lanes = lax.broadcasted_iota(jnp.int32, (1, LANES), 1)
    for local in range(per_step):
        head = pl.program_id(0) * per_step + local
        made = head_inputs(sent_ref, taps_ref, rate_ref, head, heads, place, start)
        unit_q, scale_q = unit_rows(made["q"][5])
        query = unit_q * DK ** (-0.5)
        keys, scale_k = unit_rows(made["k"][5])
        values = made["v"][5]
        beta = made["beta"]
        grad_mixed = read_rows(grad_ref, pl.multiple_of(head * DV, LANES), DV)
        decay = decay_grid(made["log"], start, rows, cols)
        strict = jnp.where(cols < rows, decay, 0.0)
        keys_keys = dot3(keys, keys, NT)
        weighted = strict * beta
        system = weighted * keys_keys
        scores = decay * dot1(query, keys, NT)
        update = update_ref[local]
        grad_scores = dot1(grad_mixed, update, NT)
        grad_update = dot1(scores, grad_mixed, TN)
        grad_targets = [None] * blocks
        for block in reversed(range(blocks)):
            at = slice(block * BLOCK, (block + 1) * BLOCK)
            right = grad_update[at]
            for later in range(block + 1, blocks):
                right = right - dot3(
                    system[later * BLOCK : (later + 1) * BLOCK, at], grad_targets[later], TN
                )
            grad_targets[block] = dot3(inverse_ref[local, block], right, TN)
        grad_target = jnp.concatenate(grad_targets, axis=0)
        grad_system = -dot1(grad_target, update, NT)
        grad_values = beta * grad_target
        grad_beta = jnp.sum(grad_target * values, axis=1, keepdims=True) + jnp.sum(
            grad_system * strict * keys_keys, axis=1, keepdims=True
        )
        grad_kk = grad_system * weighted
        grad_qk = grad_scores * decay
        grad_query = dot1(grad_qk, keys) * DK ** (-0.5)
        grad_keys = dot1(grad_kk, keys) + dot1(grad_kk, keys, TN) + dot1(grad_qk, query, TN)
        grad_spread = grad_scores * scores + grad_system * system
        lower = jnp.where(cols <= rows, 1.0, 0.0).astype(BF16)
        high, low = halves(grad_spread)
        dot = partial(lax.dot_general, dimension_numbers=TN, preferred_element_type=F32)
        after = dot(lower, high) + dot(lower, low)
        grad_log = jnp.sum(jnp.where(cols < rows, after, 0.0), axis=1, keepdims=True)
        grad_decay = grad_log * rate_ref[0, head] * sigmoid(made["decay_in"])
        grad_beta_in = grad_beta * beta * (1.0 - beta)
        lanes = made["lanes"]
        grad_pairs = jnp.where(lanes == 2 * head, grad_decay, grad_pairs)
        grad_pairs = jnp.where(lanes == 2 * head + 1, grad_beta_in, grad_pairs)
        grad_alog = jnp.sum(grad_log * made["log"], axis=0, keepdims=True)
        grad_dt = jnp.sum(grad_decay, axis=0, keepdims=True)
        small_ref[0:1] += jnp.where(small_lanes == head, grad_alog, 0.0)
        small_ref[1:2] += jnp.where(small_lanes == head, grad_dt, 0.0)
        for name, grad in (
            ("q", unit_rows_back(grad_query, made["q"][5], scale_q)),
            ("k", unit_rows_back(grad_keys, made["k"][5], scale_k)),
            ("v", grad_values),
        ):
            where, raw, taps, total, opened, _ = made[name]
            grad_raw, grad_taps = conv_silu_back(grad, total, opened, raw, taps, place, start)
            write_rows(grad_sent_ref, where, grad_raw)
            for tap in range(CONV):
                grad_taps_ref[tap : tap + 1, pl.ds(where, raw.shape[1])] += grad_taps[tap]
    write_rows(grad_sent_ref, pair_offset, grad_pairs)


def gate_forward_kernel(heads, mixed_ref, gate_ref, gain_ref, normed_ref):
    for head in range(heads):
        offset = head * DV
        mixed = read_rows(mixed_ref, offset, DV).astype(F32)
        gate = read_rows(gate_ref, offset, DV)
        scale = lax.rsqrt(jnp.mean(mixed * mixed, axis=1, keepdims=True) + EPS)
        write_rows(normed_ref, offset, mixed * scale * gain_ref[...] * (gate * sigmoid(gate)))


def gate_backward_kernel(
    heads, mixed_ref, gate_ref, gain_ref, grad_ref, grad_mixed_ref, grad_gate_ref, grad_gain_ref
):
    @pl.when(pl.program_id(0) == 0)
    def _():
        grad_gain_ref[...] = jnp.zeros_like(grad_gain_ref)

    gain = gain_ref[...]
    for head in range(heads):
        offset = head * DV
        mixed = read_rows(mixed_ref, offset, DV).astype(F32)
        gate = read_rows(gate_ref, offset, DV)
        grad = read_rows(grad_ref, offset, DV)
        scale = lax.rsqrt(jnp.mean(mixed * mixed, axis=1, keepdims=True) + EPS)
        soft = sigmoid(gate)
        plain_rows = mixed * scale
        write_rows(
            grad_gate_ref, offset, grad * plain_rows * gain * soft * (1.0 + gate * (1.0 - soft))
        )
        grad = grad * (gate * soft)
        grad_gain_ref[...] += jnp.sum(grad * plain_rows, axis=0, keepdims=True)
        grad = grad * gain
        inner = jnp.mean(mixed * grad, axis=1, keepdims=True)
        write_rows(
            grad_mixed_ref, offset, scale * grad - mixed * (scale * scale * scale * inner)
        )


def pack_kernel(query_ref, key_ref, value_ref, pairs_ref, gate_ref, out_ref):
    at = 0
    for ref in (query_ref, key_ref, value_ref, pairs_ref, gate_ref):
        block = ref[...].reshape(out_ref.shape[1], ref.shape[-1])
        out_ref[0, :, at : at + ref.shape[-1]] = block
        at += ref.shape[-1]


def pack_columns(weight, pairs, spans):
    rows = weight.shape[0]
    qw, vw = H * DK // spans, H * DV // spans
    width = 2 * qw + 2 * vw + pairs.shape[2]
    start = 2 * H * DK // vw

    def spec(columns, first):
        return pl.BlockSpec((rows, columns), lambda s: (0, first + s))

    return pl.pallas_call(
        pack_kernel,
        grid=(spans,),
        in_specs=[
            spec(qw, 0), spec(qw, spans), spec(vw, start),
            pl.BlockSpec((1, rows, pairs.shape[2]), lambda s: (s, 0, 0)),
            spec(vw, start + spans),
        ],
        out_specs=pl.BlockSpec((1, rows, width), lambda s: (s, 0, 0)),
        out_shape=jax.ShapeDtypeStruct((spans, rows, width), BF16),
        name="pack_columns",
    )(weight, weight, weight, pairs, weight)


def row_spec(array, micro):
    spans, micros, length, width = array.shape
    pick = micro if micros > 1 else 0
    return pl.BlockSpec((spans, 1, length, width), lambda h: (0, pick, 0, 0))


def span_spec(array, micro):
    _, micros, length, width = array.shape
    pick = micro if micros > 1 else 0
    return pl.BlockSpec((1, 1, length, width), lambda s: (s, pick, 0, 0))


def whole_spec(*dims):
    return pl.BlockSpec(dims, lambda h: (0,) * len(dims))


def mixer_cost(sent, heads, passes):
    count = sent.shape[0] * sent.shape[2]
    return pl.CostEstimate(
        flops=passes * heads * 2 * count * count * DV,
        bytes_accessed=passes * heads * count * count * 4,
        transcendentals=heads * count * count,
    )


def mixer_forward(micro, lengths, rates, sent, taps, heads):
    spans, _, length, width = sent.shape
    count, per_step = spans * length, 4 if heads % 4 == 0 else 1 + (heads % 2 == 0)
    blocks = count // BLOCK
    smem = pl.BlockSpec(memory_space=pltpu.SMEM)
    mixed = jax.ShapeDtypeStruct((spans, 1, length, heads * DV), BF16)
    return pl.pallas_call(
        partial(mixer_forward_kernel, micro, per_step, heads, lengths.shape[1]),
        grid=(heads // per_step,),
        in_specs=[smem, smem, row_spec(sent, micro), whole_spec(CONV, width)],
        out_specs=[
            row_spec(mixed, 0),
            pl.BlockSpec((per_step, count, DV), lambda h: (h, 0, 0)),
            pl.BlockSpec((per_step, blocks, BLOCK, BLOCK), lambda h: (h, 0, 0, 0)),
        ],
        out_shape=[
            mixed,
            jax.ShapeDtypeStruct((heads, count, DV), F32),
            jax.ShapeDtypeStruct((heads, blocks, BLOCK, BLOCK), F32),
        ],
        compiler_params=pltpu.CompilerParams(vmem_limit_bytes=40 * 1024 * 1024),
        cost_estimate=mixer_cost(sent, heads, 300),
        name="mixer_forward",
    )(lengths, rates, sent, taps)


def mixer_backward(micro, lengths, rates, sent, taps, update, inverse, grad, heads):
    spans, _, length, width = sent.shape
    count, per_step = spans * length, 2 if heads % 2 == 0 else 1
    blocks = count // BLOCK
    smem = pl.BlockSpec(memory_space=pltpu.SMEM)
    grad_sent = jax.ShapeDtypeStruct((spans, 1, length, width), BF16)
    return pl.pallas_call(
        partial(mixer_backward_kernel, micro, per_step, heads, lengths.shape[1]),
        grid=(heads // per_step,),
        in_specs=[
            smem, smem, row_spec(sent, micro), whole_spec(CONV, width),
            pl.BlockSpec((per_step, count, DV), lambda h: (h, 0, 0)),
            pl.BlockSpec((per_step, blocks, BLOCK, BLOCK), lambda h: (h, 0, 0, 0)),
            row_spec(grad, 0),
        ],
        out_specs=[row_spec(grad_sent, 0), whole_spec(CONV, width), whole_spec(8, LANES)],
        out_shape=[
            grad_sent,
            jax.ShapeDtypeStruct((CONV, width), F32),
            jax.ShapeDtypeStruct((8, LANES), F32),
        ],
        compiler_params=pltpu.CompilerParams(vmem_limit_bytes=40 * 1024 * 1024),
        cost_estimate=mixer_cost(sent, heads, 40),
        name="mixer_backward",
    )(lengths, rates, sent, taps, update, inverse, grad)


def gate_forward(micro, mixed, gate, gain, heads):
    return pl.pallas_call(
        partial(gate_forward_kernel, heads),
        grid=(mixed.shape[0],),
        in_specs=[span_spec(mixed, 0), span_spec(gate, micro), whole_spec(1, DV)],
        out_specs=span_spec(mixed, 0),
        out_shape=jax.ShapeDtypeStruct(mixed.shape, BF16),
        cost_estimate=pl.CostEstimate(
            flops=20 * mixed.size, bytes_accessed=8 * mixed.size, transcendentals=mixed.size
        ),
        name="gate_forward",
    )(mixed, gate, gain)


def gate_backward(micro, mixed, gate, gain, grad, heads):
    out = jax.ShapeDtypeStruct(mixed.shape, BF16)
    return pl.pallas_call(
        partial(gate_backward_kernel, heads),
        grid=(mixed.shape[0],),
        in_specs=[
            span_spec(mixed, 0), span_spec(gate, micro), whole_spec(1, DV), span_spec(grad, 0),
        ],
        out_specs=[span_spec(out, 0), span_spec(out, 0), whole_spec(1, DV)],
        out_shape=[out, out, jax.ShapeDtypeStruct((1, DV), F32)],
        cost_estimate=pl.CostEstimate(
            flops=40 * mixed.size, bytes_accessed=100 * mixed.size, transcendentals=mixed.size
        ),
        name="gate_backward",
    )(mixed, gate, gain, grad)


def norm_forward_kernel(base_ref, terms_ref, gain_ref, middle_ref, rows_ref):
    middle = base_ref[...].astype(F32)
    for span in range(terms_ref.shape[0]):
        middle = middle + terms_ref[span].astype(F32)
    scale = lax.rsqrt(jnp.mean(middle * middle, axis=1, keepdims=True) + EPS)
    rows = (middle * scale * gain_ref[...]).astype(BF16)
    middle_ref[...] = middle
    for span in range(rows_ref.shape[0]):
        rows_ref[span] = rows


def norm_backward_kernel(
    base_ref, middle_ref, terms_ref, gain_ref, grad_ref, rows_ref, grad_gain_ref
):
    middle = middle_ref[...]
    grad = terms_ref[0].astype(F32)
    for span in range(1, terms_ref.shape[0]):
        grad = grad + terms_ref[span].astype(F32)
    scale = lax.rsqrt(jnp.mean(middle * middle, axis=1, keepdims=True) + EPS)
    grad_gain_ref[...] = jnp.sum(middle * scale * grad, axis=0, keepdims=True)
    inner = grad * gain_ref[...]
    weight = scale * scale * scale * jnp.mean(middle * inner, axis=1, keepdims=True)
    total = base_ref[...].astype(F32) + scale * inner - middle * weight
    grad_ref[...] = total
    rows = total.astype(BF16)
    for span in range(rows_ref.shape[0]):
        rows_ref[span] = rows


def norm_forward(base, terms, gain):
    return pl.pallas_call(
        norm_forward_kernel,
        out_shape=[
            jax.ShapeDtypeStruct(base.shape, F32),
            jax.ShapeDtypeStruct(terms.shape, BF16),
        ],
        cost_estimate=pl.CostEstimate(
            flops=20 * base.size, bytes_accessed=40 * base.size, transcendentals=0
        ),
        name="norm_forward",
    )(base, terms, gain)


def norm_backward(base, middle, terms, gain):
    return pl.pallas_call(
        norm_backward_kernel,
        out_shape=[
            jax.ShapeDtypeStruct(base.shape, F32),
            jax.ShapeDtypeStruct(terms.shape, BF16),
            jax.ShapeDtypeStruct(gain.shape, F32),
        ],
        cost_estimate=pl.CostEstimate(
            flops=30 * base.size, bytes_accessed=40 * base.size, transcendentals=0
        ),
        name="norm_backward",
    )(base, middle, terms, gain)


def dot(left, right):
    return jnp.dot(left, right, preferred_element_type=F32)


def outer(left, right):
    return lax.dot_general(left, right, TN, preferred_element_type=F32)


def dot_back(left, right):
    return lax.dot_general(left, right, NT, preferred_element_type=F32)


def after(value, *earlier):
    return lax.optimization_barrier((value,) + earlier)[0]


def plain(array):
    return with_layout_constraint(array, Layout(major_to_minor=tuple(range(array.ndim))))


def exchange(blocks):
    return lax.all_to_all(blocks, "seq", split_axis=0, concat_axis=0, tiled=True)


def gather_rows(rows, *earlier):
    spans = lax.axis_size("seq")
    copies = jnp.broadcast_to(rows[None], (spans,) + rows.shape)
    return exchange(after(lax.optimization_barrier(copies), *earlier))


def scatter_rows(partial_rows, spans):
    return exchange(
        partial_rows.astype(BF16).reshape((spans, -1) + partial_rows.shape[1:])
    )


def cut(array, start, size, axis=0):
    return lax.dynamic_slice_in_dim(array, start, size, axis, allow_negative_indices=False)


def norm_scale(values):
    return lax.rsqrt(jnp.mean(values * values, axis=-1, keepdims=True) + EPS)


def norm_back(values, gain, grad):
    scale = norm_scale(values)
    inner = gain * grad
    back = scale * inner - values * (
        scale * scale * scale * jnp.mean(values * inner, axis=-1, keepdims=True)
    )
    return back, jnp.sum(values * scale * grad, axis=0)


def shards(
    tokens, lengths, in_weight, decay_weight, conv_weight, a_log, dt_bias, norm_gains, out_gain,
    out_weight, up_weight, down_weight, cotangent,
):
    spans, packs = lax.axis_size("seq"), lax.axis_size("fsdp")
    place = lax.axis_index("seq")
    micros, _, length, _ = tokens.shape
    heads = H // spans
    qw, vw, fw = heads * DK, heads * DV, FF // spans
    fp = round_up(fw, LANES)
    share = in_weight.shape[0]
    local_rows = micros * length

    def columns(array, start, count):
        return array[:, start : start + count * spans].reshape(share, spans, count)

    def widen(array, count):
        return jnp.pad(array, ((0, 0), (0, 0), (0, count - array.shape[2])))

    def by_span(pieces):
        return jnp.concatenate(pieces, axis=2).swapaxes(0, 1)

    def gather_weight(blocks):
        full = plain(lax.all_gather(plain(blocks), "fsdp", axis=1, tiled=True))
        return full.reshape(D, blocks.shape[2])

    conv_share = conv_weight.shape[0]
    conv_cols = CONV * conv_share // share
    small = jnp.concatenate([conv_weight.reshape(share, conv_cols), norm_gains.T], axis=1)
    small = jnp.broadcast_to(small[:, None], (share, spans, conv_cols + 2))
    pairs = jnp.concatenate([decay_weight.reshape(share, spans, 2 * heads), small], axis=2)
    pair_at = 2 * qw + vw
    mix_width = pair_at + LANES
    in_blocks = pack_columns(in_weight, widen(pairs, LANES).swapaxes(0, 1), spans)
    up_blocks = by_span([
        widen(columns(up_weight, 0, fw), fp),
        widen(columns(up_weight, FF, fw), fp),
    ])
    local_tokens = tokens.reshape(local_rows, D)
    local_cot = cotangent.reshape(local_rows, D)
    grouped = (spans, micros, length)
    all_rows = spans * local_rows

    in_blocks, up_blocks = lax.optimization_barrier((exchange(in_blocks), up_blocks))
    w_in = gather_weight(in_blocks)
    w_mix, w_gate = w_in[:, :mix_width], w_in[:, mix_width:]
    all_tokens = gather_rows(local_tokens, in_blocks)

    cot = gather_rows(local_cot, all_tokens).reshape(all_rows, D)
    small_at = pair_at + 2 * heads
    small = plain(w_in[:, small_at : small_at + conv_cols + 2])
    gains = small[:, conv_cols:].T.astype(F32)

    def own(base, width):
        step = conv_share // share
        rows = cut(small[:, :conv_cols], base // step + place * (width // step), width // step)
        return rows.reshape(width, CONV).T

    taps = jnp.concatenate(
        [own(0, qw), own(H * DK, qw), own(2 * H * DK, vw), jnp.zeros((CONV, LANES), BF16)],
        axis=1,
    ).astype(F32)
    rates = jnp.stack([
        -jnp.exp(cut(a_log, place * heads, heads)),
        cut(dt_bias, place * heads, heads),
    ])
    gain_row = out_gain.reshape(1, DV)
    pack_lengths = lengths[:, 0]

    inputs = all_tokens.reshape(all_rows, D).astype(F32)
    input_scale = norm_scale(inputs)
    first = (inputs * input_scale * gains[0]).astype(BF16)
    sent = dot(first, w_mix).astype(BF16)
    w_down = lax.all_gather(after(down_weight, all_tokens), "fsdp", axis=0)
    w_out = lax.all_gather(after(out_weight, all_tokens), "fsdp", axis=0, tiled=True)
    sent = sent.reshape(grouped + (mix_width,))
    mixers = []
    for micro in range(micros):
        mixers.append(
            mixer_forward(micro, pack_lengths, rates, sent, taps, heads)
        )
        sent = after(sent, mixers[-1][0])
    up_blocks = exchange(after(up_blocks, cot, mixers[0][0]))
    w_down = lax.optimization_barrier(w_down.reshape(fw, D))
    gate = dot(first, w_gate).reshape(grouped + (vw,))
    grad_act = dot_back(cot, w_down).reshape(grouped + (fw,))

    def part(array, micro):
        return array.reshape((micros, length) + array.shape[1:])[micro]

    normeds, branches, branch_rows = [], [], []
    for micro in range(micros):
        normeds.append(gate_forward(micro, mixers[micro][0], gate, gain_row, heads))
        rows = dot(normeds[-1].reshape(-1, vw), w_out).astype(BF16)
        branches.append(scatter_rows(after(rows, up_blocks), spans))
        branch_rows.append(rows)
    w_up = gather_weight(after(up_blocks, branch_rows[0]))
    middles, seconds = [], []
    for micro in range(micros):
        middle, rows = norm_forward(part(local_tokens, micro), branches[micro], gains[1:])
        middles.append(middle)
        seconds.append(exchange(rows))

    acts, grad_boths, grad_seconds, sums = [], [], [], []
    for micro in range(micros):
        seconds[micro] = after(seconds[micro], *sums)
        both = dot(seconds[micro].reshape(-1, D), w_up)
        gated, upper = both[:, :fp], both[:, fp:]
        soft = jax.nn.sigmoid(gated)
        acts.append((gated * soft * upper).astype(BF16).reshape(spans, length, fp))
        grad = jnp.pad(grad_act[:, micro].reshape(-1, fw), ((0, 0), (0, fp - fw)))
        grad_both = jnp.concatenate(
            [
                (grad * upper * soft * (1.0 + gated * (1.0 - soft))).astype(BF16),
                (grad * gated * soft).astype(BF16),
            ],
            axis=1,
        )
        grad_boths.append(grad_both.reshape(spans, length, 2 * fp))
        rows = dot_back(grad_both, w_up).astype(BF16)
        grad_seconds.append(scatter_rows(rows, spans))
        sums.append(rows)
    act = jnp.stack(acts, axis=1).reshape(all_rows, fp)[:, :fw]
    final_rows = [dot(a.reshape(-1, fp)[:, :fw], w_down).astype(BF16) for a in acts]
    down_grads = outer(after(act, act), cot).astype(BF16).reshape(packs, -1, D)
    spare = [final_rows[:1], final_rows[1:] + [down_grads]]
    grad_middles, grad_branches, grad_gain2 = [], [], 0.0
    for micro in range(micros):
        terms = after(grad_seconds[micro], *spare[min(micro, 1)])
        grad_middle, rows, grad_gain = norm_backward(
            part(local_cot, micro), middles[micro], terms, gains[1:]
        )
        grad_gain2 = grad_gain2 + grad_gain
        grad_middles.append(grad_middle)
        grad_branches.append(exchange(rows))

    def reduce_rows(grad, blocks):
        blocks = plain(grad.astype(BF16).reshape(blocks, -1, grad.shape[1]))
        return plain(lax.psum_scatter(blocks, "fsdp", scatter_dimension=1, tiled=True))

    def joined(blocks, start, width):
        return blocks[:, :, start : start + width].swapaxes(0, 1).astype(F32).reshape(share, -1)

    def all_micros(parts):
        return jnp.stack(parts, axis=1).reshape(all_rows, parts[0].shape[-1])

    up_product = outer(
        after(all_micros(seconds), grad_seconds[0], *sums), all_micros(grad_boths)
    ).astype(BF16)
    up_grads = reduce_rows(up_product, spans)
    grad_gates, grad_sents, grad_gain, grad_taps, grad_small = [], [], 0.0, 0.0, 0.0
    for micro in range(micros):
        mixed, update, inverse = mixers[micro]
        grad = after(grad_branches[micro], *grad_sents)
        grad = dot_back(grad.reshape(-1, D), w_out).reshape(spans, 1, length, vw)
        grad_mixed, grad_gate, term = gate_backward(micro, mixed, gate, gain_row, grad, heads)
        if micro + 1 == micros:
            grad_mixed = after(grad_mixed, up_grads)
        grad_sent, term_taps, term_small = mixer_backward(
            micro, pack_lengths, rates, sent, taps, update, inverse, grad_mixed, heads
        )
        grad_gates.append(grad_gate.reshape(spans, length, vw))
        grad_sents.append(grad_sent.reshape(spans, length, mix_width))
        grad_gain, grad_taps = grad_gain + term, grad_taps + term_taps
        grad_small = grad_small + term_small
    finals, wait = [], grad_sents[0]
    for micro in range(micros):
        wait = scatter_rows(after(final_rows[micro], wait), spans)
        finals.append(wait)
    block_out = jnp.stack([
        middle + jnp.sum(terms.astype(F32), axis=0) for middle, terms in zip(middles, finals)
    ]).reshape(local_rows, D)

    grad_proj = all_micros([
        jnp.concatenate(pair, axis=-1) for pair in zip(grad_sents, grad_gates)
    ])
    grad_down = lax.psum_scatter(
        after(down_grads, down_grads), "fsdp", scatter_dimension=0
    )
    in_product = outer(after(first, finals[0], up_grads), grad_proj)
    in_grads = reduce_rows(in_product, spans)
    grad_proj = after(grad_proj, in_product)
    grad_first = dot_back(grad_proj, w_in)
    grad_gain1 = jnp.sum(inputs * input_scale * grad_first, axis=0)
    first_rows = grad_first.astype(BF16)
    grad_first = scatter_rows(after(first_rows, grad_down, up_grads), spans)
    out_grads = outer(
        all_micros([n[:, 0] for n in normeds]), after(all_micros(grad_branches), first_rows)
    )
    grad_out = lax.psum_scatter(
        out_grads.astype(BF16), "fsdp", scatter_dimension=0, tiled=True
    ).astype(F32)
    gain_rows = jnp.stack([grad_gain1, grad_gain2[0]])
    flat = jnp.concatenate([
        grad_taps[:, :pair_at].reshape(-1), gain_rows.reshape(-1), grad_gain.reshape(-1),
        grad_small[:2].reshape(-1),
    ])
    flat = jnp.pad(flat, (0, round_up(flat.size, 8 * LANES) - flat.size)).reshape(-1, LANES)
    flat = lax.psum(after(flat, grad_gain1), "fsdp")
    flat = lax.all_gather(flat, "seq", axis=0).reshape(spans, -1)
    grad_norm1, _ = norm_back(
        local_tokens.astype(F32), gains[0], jnp.sum(grad_first.astype(F32), axis=0)
    )
    grad_tokens = jnp.stack(grad_middles).reshape(local_rows, D) + grad_norm1
    up_grads, flat = lax.optimization_barrier((up_grads, flat))
    up_grads = exchange(after(up_grads, grad_first))
    in_grads = exchange(after(in_grads, up_grads))
    grad_up = jnp.concatenate([joined(up_grads, 0, fw), joined(up_grads, fp, fw)], axis=1)
    grad_in = jnp.concatenate(
        [
            joined(in_grads, 0, qw),
            joined(in_grads, qw, qw),
            joined(in_grads, 2 * qw, vw),
            joined(in_grads, mix_width, vw),
        ],
        axis=1,
    )
    grad_decay = joined(in_grads, pair_at, 2 * heads)

    taps_flat = flat[:, : CONV * pair_at].reshape(spans, CONV, pair_at)

    def all_taps(start, width):
        return taps_flat[:, :, start : start + width].swapaxes(0, 1).reshape(CONV, -1)

    grad_conv = jnp.concatenate(
        [all_taps(0, qw), all_taps(qw, qw), all_taps(2 * qw, vw)], axis=1
    )
    index = place * packs + lax.axis_index("fsdp")
    grad_conv = cut(grad_conv, index * conv_share, conv_share, 1).T
    at = CONV * pair_at
    gains_flat = jnp.sum(flat[:, at : at + 2 * D], axis=0).reshape(2, D)
    gain_share = norm_gains.shape[1]
    grad_gains = cut(gains_flat, index * gain_share, gain_share, 1)
    at = at + 2 * D
    grad_gain = jnp.sum(flat[:, at : at + DV], axis=0)
    at = at + DV
    return (
        block_out.astype(BF16).reshape(micros, 1, length, D),
        grad_tokens.reshape(micros, 1, length, D),
        grad_in,
        grad_decay,
        grad_conv,
        flat[:, at : at + heads].reshape(H),
        flat[:, at + LANES : at + LANES + heads].reshape(H),
        grad_gains,
        grad_gain,
        grad_out,
        grad_up,
        grad_down.astype(F32),
    )


def solution(mesh):
    rows = P(("seq", "fsdp"), None)
    packs = P(None, "fsdp", "seq", None)
    gains = P(None, ("seq", "fsdp"))
    return jax.shard_map(
        shards,
        mesh=mesh,
        in_specs=(
            packs, P(None, "fsdp", None), rows, rows, rows, P(), P(), gains, P(), rows, rows, rows,
            packs,
        ),
        out_specs=(packs, packs, rows, rows, rows, P(), P(), gains, P(), rows, rows, rows),
        check_vma=False,
    )
```
